1024 devices in a mesh: worker: 64 (over y, z_lo, core), fsdp: 16 (over z_hi, x).
Axes of the slice: x: 4, y: 8, z: 16 (z_hi: 4, z_lo: 4; z = z_hi * 4 + z_lo), core: 2. Of those that a mesh axis runs over, the one named last changes fastest.
Arguments:
- tokens: bfloat16 [16384, 8192], P('worker', 'fsdp'), may hold values from -6 to 6
- inner_weight: bfloat16 [64, 8192, 512], P('worker', 'fsdp'), may hold values from -0.0625 to 0.0625
- key_grad: bfloat16 [16384, 512], P(('worker', 'fsdp')), may hold values from -6 to 6
- anchor: float32 [8192, 512], P('fsdp'), may hold values from -0.0625 to 0.0625
- momentum: float32 [8192, 512], P('fsdp'), may hold values from -0.06 to 0.06
- stale_delta: bfloat16 [64, 8192, 512], P('worker', 'fsdp'), may hold values from -0.29882812 to 0.29882812
Outputs:
- keys: bfloat16 [16384, 512], P(('worker', 'fsdp'))
- input_grad: bfloat16 [16384, 8192], P('worker', 'fsdp')
- new_params: bfloat16 [64, 8192, 512], P('worker', 'fsdp')
- new_momentum: float32 [8192, 512], P(('fsdp', 'worker'))
- fresh_delta: bfloat16 [64, 8192, 512], P('worker', 'fsdp')
The draws below stay inside these ranges and needn't reach their ends.
All inputs are finite; a program needn't handle non-finite values.
Results may differ from the reference program's by a relative error of at most 0.001.
Values may be sent and summed in bfloat16 or wider, within the bound.
A program may use at most 32 MiB of HBM per device.

```python
import jax
import jax.numpy as jnp
from jax import lax

D = 8192
TOK = 256
KW = 512
WORKERS = 64
TOKENS = 16384


def steps_of(stream_key, shape, shards, low, top_value):
    def one(axis_at, parts):
        heights = jax.random.uniform(jax.random.fold_in(jax.random.fold_in(stream_key, 6), axis_at), (parts,), jnp.float32, low / len(shards), top_value / len(shards))
        return jnp.repeat(jnp.exp(heights), shape[axis_at] // parts).reshape((-1,) + (1,) * (len(shape) - axis_at - 1))

    gain = one(*shards[0])
    for cut in shards[1:]:
        gain = gain * one(*cut)
    return gain


def noise(key, extent, width, bound, split=(), held_as=jnp.bfloat16):
    result = jax.random.normal(key, extent, jnp.float32) * width
    if len(split) > 0:
        result = steps_of(key, extent, split, -0.22, 0.18) * result
    return jnp.clip(result, min=-bound, max=bound).astype(held_as)


def setup_inputs(seed: int = 0) -> dict:
    key_list = jax.random.split(jax.random.key(seed), 7)
    tokens = noise(key_list[0], (TOKENS, D), 1.0, 6.0, ((0, 64), (1, 16)))
    inner_weight = noise(key_list[1], (WORKERS, D, KW), D ** -0.5, 0.0625, ((0, 64), (1, 16)))
    key_grad = noise(key_list[2], (TOKENS, KW), 1.0, 6.0, ((0, 1024),))
    anchor = noise(key_list[3], (D, KW), D ** -0.5, 0.0625, ((0, 16),), jnp.float32)
    momentum = noise(key_list[4], (D, KW), 0.01, 0.06, ((0, 16),), jnp.float32)
    stale_delta = noise(key_list[5], (WORKERS, D, KW), 0.05, 0.29882812, ((0, 64), (1, 16)))
    return dict(tokens=tokens, inner_weight=inner_weight, key_grad=key_grad, anchor=anchor, momentum=momentum, stale_delta=stale_delta)


inner_rate = 0.0005
outer_rate = 0.7
outer_momentum = 0.9


def reference(tokens, inner_weight, key_grad, anchor, momentum, stale_delta):
    summed = jnp.sum(stale_delta.astype(jnp.float32), axis=0)
    average = summed / WORKERS
    new_moment = outer_momentum * momentum + average
    common_term = average + outer_momentum * new_moment
    token_blocks = tokens.reshape(WORKERS, TOK, D)
    grad_blocks = key_grad.reshape(WORKERS, TOK, KW)

    def one_worker(operands):
        inputs, weights, upstream, stale_value = operands
        key_out = jnp.dot(inputs, weights, preferred_element_type=jnp.float32).astype(jnp.bfloat16)
        grad_weight = jnp.dot(inputs.T, upstream, preferred_element_type=jnp.float32)
        grad_input = jnp.dot(upstream, weights.T, preferred_element_type=jnp.float32).astype(jnp.bfloat16)
        fresh_term = anchor - (weights.astype(jnp.float32) - inner_rate * grad_weight)
        updated = anchor - outer_rate * (common_term + (fresh_term - stale_value.astype(jnp.float32)) / WORKERS)
        return key_out, grad_input, updated.astype(jnp.bfloat16), fresh_term.astype(jnp.bfloat16)

    key_all, grad_all, updated_all, fresh_all = lax.map(one_worker, (token_blocks, inner_weight, grad_blocks, stale_delta))
    return key_all.reshape(TOKENS, KW), grad_all.reshape(TOKENS, D), updated_all, new_moment, fresh_all
```

```python
import jax
import jax.numpy as jnp
from jax import lax
from jax.experimental import pallas as pl
from jax.experimental.pallas import tpu as pltpu
from jax.sharding import PartitionSpec as P

inner_rate = 0.0005
outer_rate = 0.7
outer_momentum = 0.9

Y, ZL, C, ZH, X = 8, 4, 2, 4, 4
WORKERS = Y * ZL * C
ROWS, KW, TOK = 512, 512, 256
HALF = ROWS // C
CH = HALF // Y
J = 2
R = CH // J
SH = 16
F32, BF16 = jnp.float32, jnp.bfloat16
MESH = pl.DeviceIdType.MESH


class Ids:
    def __init__(self):
        self.n = 0

    def __call__(self, *shape):
        first, self.n = self.n, self.n + _size(shape)

        def at(*index):
            k = 0
            for i, s in zip(index, shape):
                k = k * s + i
            return first + k

        return at


def _size(shape):
    n = 1
    for s in shape:
        n *= s
    return n


ids = Ids()
ID_PAIR = ids(Y)
ID_RS = ids(J, 2, Y // 2)
ID_Z = ids(J, ZL - 1)
ID_AG = ids(J, 2, Y // 2)
ID_PAG = ids(Y, J)
ID_KZ = ids(3)
ID_KX = ids(4, X - 1)
ID_PX = ids(X - 1)
ID_PZ = ids(3)
N_REMOTE = ids.n

loc = Ids()
L_STALE, L_W, L_TOK, L_ANCHOR, L_MOM, L_KG = (loc(1)() for _ in range(6))
L_KEYS, L_IG, L_FRESH, L_NM = (loc(1)() for _ in range(4))
L_NEW = loc(2 * Y)
N_LOCAL = loc.n


def kernel(
    tok_ref, w_ref, kg_ref, anchor_ref, mom_ref, stale_ref,
    keys_ref, ig_ref, new_ref, nm_ref, fresh_ref,
    stale, wv, tok, anchor, mom, pair, acc, rs, zbuf, full, pre,
    kg, part, xbuf, ksum, zb, ig, fbuf, nbuf, keys, nm,
    ss, rr, ls,
):
    w = lax.axis_index("worker")
    f = lax.axis_index("fsdp")
    c, zl, y = w % C, (w // C) % ZL, w // (C * ZL)
    x, zh = f % X, f // X
    d = 1 - 2 * c

    def dev(y=y, zl=zl, c=c, zh=zh, x=x):
        return ((y * ZL + zl) * C + c, zh * X + x)

    def wrap(v, n):
        return (v + n) % n

    partner = dev(c=1 - c)
    ynext = {1: dev(y=wrap(y + 1, Y)), -1: dev(y=wrap(y - 1, Y))}
    zpeer = [dev(zl=wrap(zl + k, ZL)) for k in range(1, ZL)]
    xpeer = [dev(x=wrap(x + k, X)) for k in range(1, X)]
    zfwd, zbwd = dev(zh=wrap(zh + d, ZH)), dev(zh=wrap(zh - d, ZH))

    barrier = pltpu.get_barrier_semaphore()
    peers = [partner, ynext[1], ynext[-1], *zpeer, *xpeer, zfwd, zbwd]
    for peer in peers:
        pl.semaphore_signal(barrier, inc=1, device_id=peer, device_id_type=MESH)

    def load(src, dst, at):
        copy = pltpu.make_async_copy(src, dst, ls.at[at])
        copy.start()
        return copy

    h0, h1 = pl.multiple_of(c * HALF, HALF), pl.multiple_of((1 - c) * HALF, HALF)
    c_w = load(w_ref.at[0], wv, L_W)
    c_tok = load(tok_ref, tok, L_TOK)
    c_stale = load(stale_ref.at[0], stale, L_STALE)
    c_kg = load(kg_ref, kg.at[f], L_KG)
    c_anchor = load(anchor_ref, anchor, L_ANCHOR)
    c_mom = load(mom_ref, mom, L_MOM)

    sent = []

    def send(src, dst, at, to):
        copy = pltpu.make_async_remote_copy(
            src_ref=src, dst_ref=dst, send_sem=ss.at[at], recv_sem=rr.at[at],
            device_id=to, device_id_type=MESH,
        )
        copy.start()
        sent.append(copy)

    def got(dst, at):
        pltpu.make_async_remote_copy(
            src_ref=dst, dst_ref=dst, send_sem=ss.at[at], recv_sem=rr.at[at],
            device_id=partner, device_id_type=MESH,
        ).wait_recv()

    c_w.wait()
    c_tok.wait()
    for b in range(2):
        half = jnp.dot(tok[b * 128 : b * 128 + 128, :], wv[...], preferred_element_type=F32)
        for i in range(8):
            at = b * 8 + i
            part[at % X, at // X] = half[i * SH : (i + 1) * SH]
    pl.semaphore_wait(barrier, len(peers))

    order = [Y // 2] + [s * k for k in range(Y // 2 - 1, 0, -1) for s in (1, -1)] + [0]

    def chunk(o):
        return pl.multiple_of(wrap(y + o, Y) * CH, CH)

    for i, o in enumerate(order):
        at = chunk(o)
        send(stale_ref.at[0, pl.ds(h1 + at, CH)], pair.at[pl.ds(at, CH)], ID_PAIR(i), partner)

    send(kg_ref, kg.at[f], ID_KZ(0), zfwd)
    send(kg_ref, kg.at[f], ID_KZ(1), zbwd)
    for k in range(X - 1):
        send(kg_ref, kg.at[f], ID_KX(0, k), xpeer[k])
    for k in range(X - 1):
        send(part.at[wrap(x + k + 1, X)], xbuf.at[k], ID_PX(k), xpeer[k])

    def kshare(steps):
        return wrap(zh - d * steps + 4, ZH) * X + x

    def kg_from(steps, z_id, rel):
        at = kshare(steps)
        got(kg.at[at], ID_KZ(z_id))
        for k in range(X - 1):
            send(kg.at[at], kg.at[at], ID_KX(rel, k), xpeer[k])
        return at

    c_stale.wait()

    def hops(j, way):
        return Y // 2 if (j % 2 == 0) == (way == 1) else Y // 2 - 1

    def slot(j, way, s):
        return rs.at[j, 0 if way == 1 else 1, s]

    def rid(ident, j, way, s):
        return ident(j, 0 if way == 1 else 1, s)

    long_first = [(j, way) for n in (Y // 2, Y // 2 - 1) for j in range(J) for way in (1, -1) if hops(j, way) == n]
    for i, o in enumerate(order):
        at = chunk(o)
        got(pair.at[pl.ds(at, CH)], ID_PAIR(i))
        acc[pl.ds(at, CH), :] = stale[pl.ds(h0 + at, CH), :].astype(F32) + pair[pl.ds(at, CH), :].astype(F32)
        for j, way in long_first:
            if hops(j, way) * way == o or (o == Y // 2 and hops(j, way) == o):
                send(acc.at[pl.ds(at + j * R, R)], slot(j, way, 0), rid(ID_RS, j, way, 0), ynext[way])
    for s in range(1, Y // 2):
        for j, way in long_first:
            n = hops(j, way)
            if s < n:
                mine = slot(j, way, s - 1)
                got(mine, rid(ID_RS, j, way, s - 1))
                mine[...] = mine[...] + acc[pl.ds(chunk(way * (n - s)) + j * R, R), :]
                send(mine, slot(j, way, s), rid(ID_RS, j, way, s), ynext[way])
        if s == 1:
            kg_b = kg_from(1, 0, 1)
            send(kg.at[kg_b], kg.at[kg_b], ID_KZ(2), zfwd)
            kg_from(-1, 1, 2)

    for j in range(J):
        total = acc[pl.ds(chunk(0) + j * R, R), :]
        for way in (1, -1):
            n = hops(j, way)
            got(slot(j, way, n - 1), rid(ID_RS, j, way, n - 1))
            total = total + slot(j, way, n - 1)[...]
        zbuf[j, zl] = total
        for k in range(ZL - 1):
            send(zbuf.at[j, zl], zbuf.at[j, zl], ID_Z(j, k), zpeer[k])

    kg_from(2, 2, 3)
    for k in range(X - 1):
        got(xbuf.at[k], ID_PX(k))
    for i in range(ZH):
        ksum[i] = (part[x, i] + xbuf[0, i]) + (xbuf[1, i] + xbuf[2, i])
    send(ksum.at[wrap(zh + 2, ZH)], zb.at[0], ID_PZ(0), zfwd)
    send(ksum.at[wrap(zh - d, ZH)], zb.at[1], ID_PZ(1), zbwd)

    for rel, steps in enumerate((0, 1, -1, 2)):
        for k in range(X - 1):
            at = wrap(zh - d * steps + 4, ZH) * X + wrap(x - k - 1, X)
            got(kg.at[at], ID_KX(rel, k))
    c_kg.wait()
    portion = kg[...].reshape(TOK, KW)
    for b in range(2):
        ig[b * 128 : b * 128 + 128, :] = lax.dot_general(
            portion[b * 128 : b * 128 + 128], wv[...], (((1,), (1,)), ((), ())), preferred_element_type=F32
        ).astype(BF16)
    c_ig = load(ig, ig_ref, L_IG)
    c_anchor.wait()
    c_mom.wait()
    for b in range(4):
        rows = slice(b * 128, b * 128 + 128)
        grad = lax.dot_general(
            tok[:, rows], portion, (((0,), (0,)), ((), ())), preferred_element_type=F32
        )
        fresh = anchor[rows, :] - (wv[rows, :].astype(F32) - inner_rate * grad)
        fbuf[rows, :] = fresh.astype(BF16)
        pre[rows, :] = anchor[rows, :] - outer_rate * (
            outer_momentum * outer_momentum * mom[rows, :] + (fresh - stale[rows, :].astype(F32)) * (1.0 / WORKERS)
        )
    c_fresh = load(fbuf, fresh_ref.at[0], L_FRESH)

    def place(core, o, j):
        return pl.ds(pl.multiple_of(core * HALF + chunk(o) + j * R, R), R)

    for j in range(J):
        for k in range(ZL - 1):
            got(zbuf.at[j, wrap(zl - k - 1, ZL)], ID_Z(j, k))
        here = place(c, 0, j)
        full[here, :] = ((zbuf[j, 0] + zbuf[j, 1]) + (zbuf[j, 2] + zbuf[j, 3])) * (1.0 / WORKERS)
        for way in (1, -1):
            send(full.at[here], full.at[here], rid(ID_AG, j, way, 0), ynext[way])
        send(full.at[here], full.at[here], ID_PAG(0, j), partner)

    outs = []

    def finish(core, o, n):
        rows = pl.ds(pl.multiple_of(core * HALF + chunk(o), CH), CH)
        nbuf[rows, :] = (pre[rows, :] - (outer_rate * (1.0 + outer_momentum)) * full[rows, :]).astype(BF16)
        outs.append(load(nbuf.at[rows], new_ref.at[0, rows], L_NEW(n)))

    finish(c, 0, 0)
    for s in range(Y // 2):
        for j, way in long_first:
            n = hops(j, way)
            if s < n:
                o = -way * (s + 1)
                here = place(c, o, j)
                got(full.at[here], rid(ID_AG, j, way, s))
                if s + 1 < n:
                    send(full.at[here], full.at[here], rid(ID_AG, j, way, s + 1), ynext[way])
                send(full.at[here], full.at[here], ID_PAG(o % Y, j), partner)
        if s == 0:
            got(zb.at[0], ID_PZ(0))
            zb[0] = zb[0] + ksum[wrap(zh + d, ZH)]
            send(zb.at[0], zb.at[2], ID_PZ(2), zfwd)
        for o in (s + 1, -s - 1) if s + 1 < Y // 2 else (s + 1,):
            finish(c, o, o % Y)
        for o in (s, -s) if s else (0,):
            for j in range(J):
                got(full.at[place(1 - c, o, j)], ID_PAG(o % Y, j))
            finish(1 - c, o, Y + o % Y)
    got(zb.at[1], ID_PZ(1))
    got(zb.at[2], ID_PZ(2))
    keys[...] = (ksum[zh] + (zb[1] + zb[2])).astype(BF16)
    c_keys = load(keys, keys_ref, L_KEYS)
    for j in range(J):
        got(full.at[place(1 - c, Y // 2, j)], ID_PAG(Y // 2, j))
    finish(1 - c, Y // 2, Y + Y // 2)
    share = pl.ds(pl.multiple_of(w * 8, 8), 8)
    nm[...] = outer_momentum * mom[share, :] + full[share, :]
    c_nm = load(nm, nm_ref, L_NM)

    for copy in sent:
        copy.wait_send()
    for copy in (c_ig, c_fresh, c_keys, c_nm, *outs):
        copy.wait()


def local(*args):
    scratch = [
        pltpu.VMEM((ROWS, KW), BF16),
        pltpu.VMEM((ROWS, KW), BF16),
        pltpu.VMEM((TOK, ROWS), BF16),
        pltpu.VMEM((ROWS, KW), F32),
        pltpu.VMEM((ROWS, KW), F32),
        pltpu.VMEM((HALF, KW), BF16),
        pltpu.VMEM((HALF, KW), F32),
        pltpu.VMEM((J, 2, Y // 2, R, KW), F32),
        pltpu.VMEM((J, ZL, R, KW), F32),
        pltpu.VMEM((ROWS, KW), F32),
        pltpu.VMEM((ROWS, KW), F32),
        pltpu.VMEM((ZH * X, SH, KW), BF16),
        pltpu.VMEM((X, ZH, SH, KW), F32),
        pltpu.VMEM((X - 1, ZH, SH, KW), F32),
        pltpu.VMEM((ZH, SH, KW), F32),
        pltpu.VMEM((3, SH, KW), F32),
        pltpu.VMEM((TOK, ROWS), BF16),
        pltpu.VMEM((ROWS, KW), BF16),
        pltpu.VMEM((ROWS, KW), BF16),
        pltpu.VMEM((SH, KW), BF16),
        pltpu.VMEM((8, KW), F32),
        pltpu.SemaphoreType.DMA((N_REMOTE,)),
        pltpu.SemaphoreType.DMA((N_REMOTE,)),
        pltpu.SemaphoreType.DMA((N_LOCAL,)),
    ]
    hbm = pl.BlockSpec(memory_space=pl.ANY)
    return pl.pallas_call(
        kernel,
        out_shape=(
            jax.ShapeDtypeStruct((SH, KW), BF16),
            jax.ShapeDtypeStruct((TOK, ROWS), BF16),
            jax.ShapeDtypeStruct((1, ROWS, KW), BF16),
            jax.ShapeDtypeStruct((8, KW), F32),
            jax.ShapeDtypeStruct((1, ROWS, KW), BF16),
        ),
        in_specs=[hbm] * 6,
        out_specs=(hbm,) * 5,
        scratch_shapes=scratch,
        compiler_params=pltpu.CompilerParams(
            collective_id=0, has_side_effects=True, vmem_limit_bytes=60 * 1024 * 1024
        ),
    )(*args)


def solution(mesh):
    in_specs = (
        P("worker", "fsdp"),
        P("worker", "fsdp", None),
        P(("worker", "fsdp"), None),
        P("fsdp", None),
        P("fsdp", None),
        P("worker", "fsdp", None),
    )
    out_specs = (
        P(("worker", "fsdp"), None),
        P("worker", "fsdp"),
        P("worker", "fsdp", None),
        P(("fsdp", "worker"), None),
        P("worker", "fsdp", None),
    )
    return jax.shard_map(local, mesh=mesh, in_specs=in_specs, out_specs=out_specs, check_vma=False)
```

```python
import jax
import jax.numpy as jnp
from jax import lax
from jax.experimental import pallas as pl
from jax.experimental.pallas import tpu as pltpu
from jax.sharding import PartitionSpec as P

inner_rate = 0.0005
outer_rate = 0.7
outer_momentum = 0.9

Y, ZL, C, ZH, X = 8, 4, 2, 4, 4
WORKERS = Y * ZL * C
ROWS, KW, TOK = 512, 512, 256
HALF = ROWS // C
CH = HALF // Y
J = 2
R = CH // J
SH = 16
VMEM_LIMIT = 53400 * 1024
F32, BF16 = jnp.float32, jnp.bfloat16
MESH = pl.DeviceIdType.MESH


class Ids:
    def __init__(self):
        self.n = 0

    def __call__(self, *shape):
        first, self.n = self.n, self.n + _size(shape)

        def at(*index):
            k = 0
            for i, s in zip(index, shape):
                k = k * s + i
            return first + k

        return at


def _size(shape):
    n = 1
    for s in shape:
        n *= s
    return n


ids = Ids()
ID_PAIR = ids(Y)
ID_RS = ids(J, 2, Y // 2)
ID_Z = ids(J, ZL - 1)
ID_AG = ids(J, 2, Y // 2)
ID_PAG = ids(Y, J)
ID_KZ = ids(ZH - 1)
ID_KX = ids(4, X - 1)
ID_PX = ids(X - 1)
ID_PZ = ids(ZH - 1)
N_REMOTE = ids.n

loc = Ids()
L_STALE, L_W, L_TOK, L_ANCHOR, L_MOM, L_KG = (loc(1)() for _ in range(6))
N_LOCAL = loc.n


def kernel(
    tok_ref, w_ref, kg_ref, anchor_ref, mom_ref, stale_ref,
    keys, ig, nbuf, nm, fbuf,
    stale, wv, tok, anchor, mom, pair, acc, rs, zbuf, full, pre,
    kg, part, xbuf, ksum, zb,
    ss, rr, ls, entered,
):
    w = lax.axis_index("worker")
    f = lax.axis_index("fsdp")
    c, zl, y = w % C, (w // C) % ZL, w // (C * ZL)
    x, zh = f % X, f // X

    def dev(y=y, zl=zl, c=c, zh=zh, x=x):
        return ((y * ZL + zl) * C + c, zh * X + x)

    def wrap(v, n):
        return (v + n) % n

    partner = dev(c=1 - c)
    ynext = {1: dev(y=wrap(y + 1, Y)), -1: dev(y=wrap(y - 1, Y))}
    zpeer = [dev(zl=wrap(zl + k, ZL)) for k in range(1, ZL)]
    xpeer = [dev(x=wrap(x + k, X)) for k in range(1, X)]

    column = y + zl + c + x

    def rank(zh):
        return 2 * zh + jnp.where(column + zh == 0, 5, 0)

    others = [wrap(zh + k, ZH) for k in range(1, ZH)]
    hpeer = [dev(zh=at) for at in others]
    lower = [rank(at) < rank(zh) for at in others]
    n_lower = sum(jnp.where(low, 1, 0) for low in lower)

    barrier = pltpu.get_barrier_semaphore()
    peers = [partner, ynext[1], ynext[-1], *zpeer, *xpeer]
    for peer in peers:
        pl.semaphore_signal(barrier, inc=1, device_id=peer, device_id_type=MESH)
    for k in range(ZH - 1):

        @pl.when(jnp.logical_not(lower[k]))
        def _():
            pl.semaphore_signal(barrier, inc=1, device_id=hpeer[k], device_id_type=MESH)

    def load(src, dst, at):
        copy = pltpu.make_async_copy(src, dst, ls.at[at])
        copy.start()
        return copy

    h0, h1 = pl.multiple_of(c * HALF, HALF), pl.multiple_of((1 - c) * HALF, HALF)
    c_stale = load(stale_ref.at[0], stale, L_STALE)
    c_w = load(w_ref.at[0], wv, L_W)
    c_tok = load(tok_ref, tok, L_TOK)
    c_kg = load(kg_ref, kg.at[f], L_KG)
    c_anchor = load(anchor_ref, anchor, L_ANCHOR)
    c_mom = load(mom_ref, mom, L_MOM)

    sent = []

    def send(src, dst, at, to):
        copy = pltpu.make_async_remote_copy(
            src_ref=src, dst_ref=dst, send_sem=ss.at[at], recv_sem=rr.at[at],
            device_id=to, device_id_type=MESH,
        )
        copy.start()
        sent.append(copy)

    def got(dst, at):
        pltpu.make_async_remote_copy(
            src_ref=dst, dst_ref=dst, send_sem=ss.at[at], recv_sem=rr.at[at],
            device_id=partner, device_id_type=MESH,
        ).wait_recv()

    pl.semaphore_wait(barrier, len(peers) + n_lower)

    order = [Y // 2] + [s * k for k in range(Y // 2 - 1, 0, -1) for s in (1, -1)] + [0]

    def chunk(o):
        return pl.multiple_of(wrap(y + o, Y) * CH, CH)

    for i, o in enumerate(order):
        at = chunk(o)
        send(stale_ref.at[0, pl.ds(h1 + at, CH)], pair.at[pl.ds(at, CH)], ID_PAIR(i), partner)

    c_stale.wait()

    def hops(j, way):
        return Y // 2 if (j % 2 == 0) == (way == 1) else Y // 2 - 1

    def slot(j, way, s):
        return rs.at[j, 0 if way == 1 else 1, s]

    def rid(ident, j, way, s):
        return ident(j, 0 if way == 1 else 1, s)

    long_first = [(j, way) for n in (Y // 2, Y // 2 - 1) for j in range(J) for way in (1, -1) if hops(j, way) == n]
    for i, o in enumerate(order):
        at = chunk(o)
        got(pair.at[pl.ds(at, CH)], ID_PAIR(i))
        acc[pl.ds(at, CH), :] = stale[pl.ds(h0 + at, CH), :].astype(F32) + pair[pl.ds(at, CH), :].astype(F32)
        for j, way in long_first:
            if hops(j, way) * way == o or (o == Y // 2 and hops(j, way) == o):
                send(acc.at[pl.ds(at + j * R, R)], slot(j, way, 0), rid(ID_RS, j, way, 0), ynext[way])

    def kz(k):
        copy = pltpu.make_async_remote_copy(
            src_ref=kg_ref, dst_ref=kg.at[f], send_sem=ss.at[ID_KZ(k)], recv_sem=rr.at[ID_KZ(k)],
            device_id=hpeer[k], device_id_type=MESH,
        )
        return copy

    for k in range(ZH - 1):

        @pl.when(lower[k])
        def _():
            pl.semaphore_signal(entered, inc=1, device_id=hpeer[k], device_id_type=MESH)
            kz(k).start()

        sent.append(kz(k))
    for k in range(X - 1):
        send(kg_ref, kg.at[f], ID_KX(0, k), xpeer[k])

    c_w.wait()
    c_tok.wait()
    for b in range(2):
        half = jnp.dot(tok[b * 128 : b * 128 + 128, :], wv[...], preferred_element_type=F32)
        for i in range(8):
            at = b * 8 + i
            part[at % X, at // X] = half[i * SH : (i + 1) * SH]
    for k in range(X - 1):
        send(part.at[wrap(x + k + 1, X)], xbuf.at[k], ID_PX(k), xpeer[k])

    for s in range(1, Y // 2):
        for j, way in long_first:
            n = hops(j, way)
            if s < n:
                mine = slot(j, way, s - 1)
                got(mine, rid(ID_RS, j, way, s - 1))
                mine[...] = mine[...] + acc[pl.ds(chunk(way * (n - s)) + j * R, R), :]
                send(mine, slot(j, way, s), rid(ID_RS, j, way, s), ynext[way])

    for j in range(J):
        total = acc[pl.ds(chunk(0) + j * R, R), :]
        for way in (1, -1):
            n = hops(j, way)
            got(slot(j, way, n - 1), rid(ID_RS, j, way, n - 1))
            total = total + slot(j, way, n - 1)[...]
        zbuf[j, zl] = total
        for k in range(ZL - 1):
            send(zbuf.at[j, zl], zbuf.at[j, zl], ID_Z(j, k), zpeer[k])

    for k in range(X - 1):
        got(xbuf.at[k], ID_PX(k))
    for i in range(ZH):
        ksum[i] = (part[x, i] + xbuf[0, i]) + (xbuf[1, i] + xbuf[2, i])

    @pl.when(n_lower < ZH - 1)
    def _():
        pl.semaphore_wait(entered, ZH - 1 - n_lower)

    for k in range(ZH - 1):

        @pl.when(jnp.logical_not(lower[k]))
        def _():
            kz(k).start()

    for k in range(ZH - 1):
        send(ksum.at[others[k]], zb.at[k], ID_PZ(k), hpeer[k])
    for k in range(ZH - 1):
        at = wrap(zh - k - 1, ZH) * X + x
        got(kg.at[at], ID_KZ(k))
        for i in range(X - 1):
            send(kg.at[at], kg.at[at], ID_KX(k + 1, i), xpeer[i])

    def place(core, o, j):
        return pl.ds(pl.multiple_of(core * HALF + chunk(o) + j * R, R), R)

    for j in range(J):
        for k in range(ZL - 1):
            got(zbuf.at[j, wrap(zl - k - 1, ZL)], ID_Z(j, k))
        here = place(c, 0, j)
        full[here, :] = ((zbuf[j, 0] + zbuf[j, 1]) + (zbuf[j, 2] + zbuf[j, 3])) * (1.0 / WORKERS)
        for way in (1, -1):
            send(full.at[here], full.at[here], rid(ID_AG, j, way, 0), ynext[way])
        send(full.at[here], full.at[here], ID_PAG(0, j), partner)

    for rel in range(ZH):
        for k in range(X - 1):
            at = wrap(zh - rel, ZH) * X + wrap(x - k - 1, X)
            got(kg.at[at], ID_KX(rel, k))
    c_kg.wait()
    portion = kg[...].reshape(TOK, KW)
    for b in range(2):
        ig[b * 128 : b * 128 + 128, :] = lax.dot_general(
            portion[b * 128 : b * 128 + 128], wv[...], (((1,), (1,)), ((), ())), preferred_element_type=F32
        ).astype(BF16)
    c_anchor.wait()
    c_mom.wait()
    for b in range(4):
        rows = slice(b * 128, b * 128 + 128)
        grad = lax.dot_general(
            tok[:, rows], portion, (((0,), (0,)), ((), ())), preferred_element_type=F32
        )
        fresh = anchor[rows, :] - (wv[rows, :].astype(F32) - inner_rate * grad)
        fbuf[0, rows, :] = fresh.astype(BF16)
        pre[rows, :] = anchor[rows, :] - outer_rate * (
            outer_momentum * outer_momentum * mom[rows, :] + (fresh - stale[rows, :].astype(F32)) * (1.0 / WORKERS)
        )

    def finish(core, o):
        rows = pl.ds(pl.multiple_of(core * HALF + chunk(o), CH), CH)
        nbuf[0, rows, :] = (pre[rows, :] - (outer_rate * (1.0 + outer_momentum)) * full[rows, :]).astype(BF16)

    finish(c, 0)
    for s in range(Y // 2):
        for j, way in long_first:
            n = hops(j, way)
            if s < n:
                o = -way * (s + 1)
                here = place(c, o, j)
                got(full.at[here], rid(ID_AG, j, way, s))
                if s + 1 < n:
                    send(full.at[here], full.at[here], rid(ID_AG, j, way, s + 1), ynext[way])
                send(full.at[here], full.at[here], ID_PAG(o % Y, j), partner)
        for o in (s + 1, -s - 1) if s + 1 < Y // 2 else (s + 1,):
            finish(c, o)
        for o in (s, -s) if s else (0,):
            for j in range(J):
                got(full.at[place(1 - c, o, j)], ID_PAG(o % Y, j))
            finish(1 - c, o)
    for k in range(ZH - 1):
        got(zb.at[k], ID_PZ(k))
    keys[...] = ((ksum[zh] + zb[0]) + (zb[1] + zb[2])).astype(BF16)
    for j in range(J):
        got(full.at[place(1 - c, Y // 2, j)], ID_PAG(Y // 2, j))
    finish(1 - c, Y // 2)
    share = pl.ds(pl.multiple_of(w * 8, 8), 8)
    nm[...] = outer_momentum * mom[share, :] + full[share, :]

    for copy in sent:
        copy.wait_send()


def write(*refs):
    n = len(refs) // 2
    copies = [pltpu.make_async_copy(a, b, refs[-1].at[i]) for i, (a, b) in enumerate(zip(refs[:n], refs[n:-1]))]
    for copy in copies:
        copy.start()
    for copy in copies:
        copy.wait()


def local(*args):
    scratch = [
        pltpu.VMEM((ROWS, KW), BF16),
        pltpu.VMEM((ROWS, KW), BF16),
        pltpu.VMEM((TOK, ROWS), BF16),
        pltpu.VMEM((ROWS, KW), F32),
        pltpu.VMEM((ROWS, KW), F32),
        pltpu.VMEM((HALF, KW), BF16),
        pltpu.VMEM((HALF, KW), F32),
        pltpu.VMEM((J, 2, Y // 2, R, KW), F32),
        pltpu.VMEM((J, ZL, R, KW), F32),
        pltpu.VMEM((ROWS, KW), F32),
        pltpu.VMEM((ROWS, KW), F32),
        pltpu.VMEM((ZH * X, SH, KW), BF16),
        pltpu.VMEM((X, ZH, SH, KW), F32),
        pltpu.VMEM((X - 1, ZH, SH, KW), F32),
        pltpu.VMEM((ZH, SH, KW), F32),
        pltpu.VMEM((3, SH, KW), F32),
        pltpu.SemaphoreType.DMA((N_REMOTE,)),
        pltpu.SemaphoreType.DMA((N_REMOTE,)),
        pltpu.SemaphoreType.DMA((N_LOCAL,)),
        pltpu.SemaphoreType.REGULAR,
    ]
    hbm = pl.BlockSpec(memory_space=pl.ANY)
    vmem = pl.BlockSpec(memory_space=pltpu.VMEM)
    shapes = (
        jax.ShapeDtypeStruct((SH, KW), BF16),
        jax.ShapeDtypeStruct((TOK, ROWS), BF16),
        jax.ShapeDtypeStruct((1, ROWS, KW), BF16),
        jax.ShapeDtypeStruct((8, KW), F32),
        jax.ShapeDtypeStruct((1, ROWS, KW), BF16),
    )
    results = pl.pallas_call(
        kernel,
        out_shape=shapes,
        in_specs=[hbm] * 6,
        out_specs=(vmem,) * 5,
        scratch_shapes=scratch,
        compiler_params=pltpu.CompilerParams(
            collective_id=0, has_side_effects=True, vmem_limit_bytes=VMEM_LIMIT
        ),
    )(*args)
    return pl.pallas_call(
        write,
        out_shape=shapes,
        in_specs=[vmem] * 5,
        out_specs=(hbm,) * 5,
        scratch_shapes=[pltpu.SemaphoreType.DMA((5,))],
        compiler_params=pltpu.CompilerParams(vmem_limit_bytes=4 * 1024 * 1024),
    )(*results)


def solution(mesh):
    in_specs = (
        P("worker", "fsdp"),
        P("worker", "fsdp", None),
        P(("worker", "fsdp"), None),
        P("fsdp", None),
        P("fsdp", None),
        P("worker", "fsdp", None),
    )
    out_specs = (
        P(("worker", "fsdp"), None),
        P("worker", "fsdp"),
        P("worker", "fsdp", None),
        P(("fsdp", "worker"), None),
        P("worker", "fsdp", None),
    )
    return jax.shard_map(local, mesh=mesh, in_specs=in_specs, out_specs=out_specs, check_vma=False)
```

```python
import jax
import jax.numpy as jnp
from jax import lax
from jax.experimental import pallas as pl
from jax.experimental.pallas import tpu as pltpu
from jax.sharding import PartitionSpec as P

inner_rate = 0.0005
outer_rate = 0.7
outer_momentum = 0.9

Y, ZL, C, ZH, X = 8, 4, 2, 4, 4
WORKERS = Y * ZL * C
ROWS, KW, TOK = 512, 512, 256
HALF = ROWS // C
CH = HALF // Y
J = 2
R = CH // J
SH = 16
VMEM_LIMIT = 40 * 1024 * 1024
F32, BF16 = jnp.float32, jnp.bfloat16
MESH = pl.DeviceIdType.MESH


class Ids:
    def __init__(self):
        self.n = 0

    def __call__(self, *shape):
        first, self.n = self.n, self.n + _size(shape)

        def at(*index):
            k = 0
            for i, s in zip(index, shape):
                k = k * s + i
            return first + k

        return at


def _size(shape):
    n = 1
    for s in shape:
        n *= s
    return n


ids = Ids()
ID_PAIR = ids(Y)
ID_RS = ids(J, 2, Y // 2)
ID_Z = ids(J, ZL - 1)
ID_AG = ids(J, 2, Y // 2)
ID_PAG = ids(Y, J)
ID_KZ = ids(ZH - 1)
ID_KX = ids(4, X - 1)
ID_PX = ids(X - 1)
ID_PZ = ids(ZH - 1)
N_REMOTE = ids.n

loc = Ids()
L_STALE, L_W, L_TOK, L_ANCHOR, L_MOM, L_KG = (loc(1)() for _ in range(6))
N_LOCAL = loc.n


def kernel(
    tok_ref, w_ref, kg_ref, anchor_ref, mom_ref, stale_ref,
    keys, ig, nbuf, nm, fbuf,
    stale, wv, tok, anchor, mom, pair, acc, rs, zbuf, full, pre,
    kg, part, xbuf, ksum, zb,
    ss, rr, ls, ans_c, ans_y, ans_z, ans_x, ans_h,
):
    w = lax.axis_index("worker")
    f = lax.axis_index("fsdp")
    c, zl, y = w % C, (w // C) % ZL, w // (C * ZL)
    x, zh = f % X, f // X

    def dev(y=y, zl=zl, c=c, zh=zh, x=x):
        return ((y * ZL + zl) * C + c, zh * X + x)

    def wrap(v, n):
        return (v + n) % n

    partner = dev(c=1 - c)
    ynext = {1: dev(y=wrap(y + 1, Y)), -1: dev(y=wrap(y - 1, Y))}
    zpeer = [dev(zl=wrap(zl + k, ZL)) for k in range(1, ZL)]
    xpeer = [dev(x=wrap(x + k, X)) for k in range(1, X)]

    zat = [wrap(zl + k, ZL) for k in range(1, ZL)]
    xat = [wrap(x + k, X) for k in range(1, X)]
    hat = [wrap(zh + k, ZH) for k in range(1, ZH)]
    hpeer = [dev(zh=at) for at in hat]
    lower = [at < zh for at in hat]

    odd = y % 2 == 1
    relations = [(partner, c == 1, ans_c)]
    relations += [(ynext[way], odd, ans_y.at[0 if way == -1 else 1]) for way in (1, -1)]
    relations += [(peer, at < zl, ans_z) for peer, at in zip(zpeer, zat)]
    relations += [(peer, at < x, ans_x) for peer, at in zip(xpeer, xat)]
    relations += [(peer, at > zh, ans_h) for peer, at in zip(hpeer, hat)]
    n_greeted = (1 - c) + 2 * (1 - y % 2) + (ZL - 1 - zl) + (X - 1 - x) + zh

    barrier = pltpu.get_barrier_semaphore()
    for peer, greets, _ in relations:

        @pl.when(greets)
        def _():
            pl.semaphore_signal(barrier, inc=1, device_id=peer, device_id_type=MESH)

    def enter():
        @pl.when(n_greeted > 0)
        def _():
            pl.semaphore_wait(barrier, n_greeted)

        for peer, greets, answer in relations:

            @pl.when(jnp.logical_not(greets))
            def _():
                pl.semaphore_signal(answer, inc=1, device_id=peer, device_id_type=MESH)

    def answered(sem, n):
        @pl.when(n > 0)
        def _():
            pl.semaphore_wait(sem, n)

    def load(src, dst, at):
        copy = pltpu.make_async_copy(src, dst, ls.at[at])
        copy.start()
        return copy

    h0, h1 = pl.multiple_of(c * HALF, HALF), pl.multiple_of((1 - c) * HALF, HALF)
    c_stale = load(stale_ref.at[0], stale, L_STALE)
    c_w = load(w_ref.at[0], wv, L_W)
    c_tok = load(tok_ref, tok, L_TOK)
    c_kg = load(kg_ref, kg.at[f], L_KG)
    c_anchor = load(anchor_ref, anchor, L_ANCHOR)
    c_mom = load(mom_ref, mom, L_MOM)

    sent = []

    def send(src, dst, at, to):
        copy = pltpu.make_async_remote_copy(
            src_ref=src, dst_ref=dst, send_sem=ss.at[at], recv_sem=rr.at[at],
            device_id=to, device_id_type=MESH,
        )
        copy.start()
        sent.append(copy)

    def got(dst, at):
        pltpu.make_async_remote_copy(
            src_ref=dst, dst_ref=dst, send_sem=ss.at[at], recv_sem=rr.at[at],
            device_id=partner, device_id_type=MESH,
        ).wait_recv()

    enter()
    answered(ans_c, c)

    order = [Y // 2] + [s * k for k in range(Y // 2 - 1, 0, -1) for s in (1, -1)] + [0]

    def chunk(o):
        return pl.multiple_of(wrap(y + o, Y) * CH, CH)

    for i, o in enumerate(order):
        at = chunk(o)
        send(stale_ref.at[0, pl.ds(h1 + at, CH)], pair.at[pl.ds(at, CH)], ID_PAIR(i), partner)

    c_stale.wait()

    def hops(j, way):
        return Y // 2 if (j % 2 == 0) == (way == 1) else Y // 2 - 1

    def slot(j, way, s):
        return rs.at[j, 0 if way == 1 else 1, s]

    def rid(ident, j, way, s):
        return ident(j, 0 if way == 1 else 1, s)

    long_first = [(j, way) for n in (Y // 2, Y // 2 - 1) for j in range(J) for way in (1, -1) if hops(j, way) == n]
    ways = [1, -1]
    for i, o in enumerate(order):
        at = chunk(o)
        got(pair.at[pl.ds(at, CH)], ID_PAIR(i))
        acc[pl.ds(at, CH), :] = stale[pl.ds(h0 + at, CH), :].astype(F32) + pair[pl.ds(at, CH), :].astype(F32)
        for j, way in long_first:
            if hops(j, way) * way == o or (o == Y // 2 and hops(j, way) == o):
                if way in ways:
                    ways.remove(way)
                    answered(ans_y.at[0 if way == 1 else 1], y % 2)
                send(acc.at[pl.ds(at + j * R, R)], slot(j, way, 0), rid(ID_RS, j, way, 0), ynext[way])

    def kz(k):
        copy = pltpu.make_async_remote_copy(
            src_ref=kg_ref, dst_ref=kg.at[f], send_sem=ss.at[ID_KZ(k)], recv_sem=rr.at[ID_KZ(k)],
            device_id=hpeer[k], device_id_type=MESH,
        )
        return copy

    for k in range(ZH - 1):

        @pl.when(lower[k])
        def _():
            kz(k).start()

        sent.append(kz(k))

    c_w.wait()
    c_tok.wait()
    for b in range(2):
        half = jnp.dot(tok[b * 128 : b * 128 + 128, :], wv[...], preferred_element_type=F32)
        for i in range(8):
            at = b * 8 + i
            part[at % X, at // X] = half[i * SH : (i + 1) * SH]

    for s in range(1, Y // 2):
        for j, way in long_first:
            n = hops(j, way)
            if s < n:
                mine = slot(j, way, s - 1)
                got(mine, rid(ID_RS, j, way, s - 1))
                mine[...] = mine[...] + acc[pl.ds(chunk(way * (n - s)) + j * R, R), :]
                send(mine, slot(j, way, s), rid(ID_RS, j, way, s), ynext[way])
        if s == 1:
            answered(ans_x, x)
            for k in range(X - 1):
                send(kg_ref, kg.at[f], ID_KX(0, k), xpeer[k])
            for k in range(X - 1):
                send(part.at[xat[k]], xbuf.at[k], ID_PX(k), xpeer[k])

    answered(ans_z, zl)
    for j in range(J):
        total = acc[pl.ds(chunk(0) + j * R, R), :]
        for way in (1, -1):
            n = hops(j, way)
            got(slot(j, way, n - 1), rid(ID_RS, j, way, n - 1))
            total = total + slot(j, way, n - 1)[...]
        zbuf[j, zl] = total
        for k in range(ZL - 1):
            send(zbuf.at[j, zl], zbuf.at[j, zl], ID_Z(j, k), zpeer[k])

    for k in range(X - 1):
        got(xbuf.at[k], ID_PX(k))
    for i in range(ZH):
        ksum[i] = (part[x, i] + xbuf[0, i]) + (xbuf[1, i] + xbuf[2, i])
    answered(ans_h, ZH - 1 - zh)
    for k in range(ZH - 1):

        @pl.when(jnp.logical_not(lower[k]))
        def _():
            kz(k).start()

    for k in range(ZH - 1):
        send(ksum.at[hat[k]], zb.at[k], ID_PZ(k), hpeer[k])
    for k in range(ZH - 1):
        at = wrap(zh - k - 1, ZH) * X + x
        got(kg.at[at], ID_KZ(k))
        for i in range(X - 1):
            send(kg.at[at], kg.at[at], ID_KX(k + 1, i), xpeer[i])

    def place(core, o, j):
        return pl.ds(pl.multiple_of(core * HALF + chunk(o) + j * R, R), R)

    for j in range(J):
        for k in range(ZL - 1):
            got(zbuf.at[j, wrap(zl - k - 1, ZL)], ID_Z(j, k))
        here = place(c, 0, j)
        full[here, :] = ((zbuf[j, 0] + zbuf[j, 1]) + (zbuf[j, 2] + zbuf[j, 3])) * (1.0 / WORKERS)
        for way in (1, -1):
            send(full.at[here], full.at[here], rid(ID_AG, j, way, 0), ynext[way])
        send(full.at[here], full.at[here], ID_PAG(0, j), partner)

    for rel in range(ZH):
        for k in range(X - 1):
            at = wrap(zh - rel, ZH) * X + wrap(x - k - 1, X)
            got(kg.at[at], ID_KX(rel, k))
    c_kg.wait()
    portion = kg[...].reshape(TOK, KW)
    for b in range(2):
        ig[b * 128 : b * 128 + 128, :] = lax.dot_general(
            portion[b * 128 : b * 128 + 128], wv[...], (((1,), (1,)), ((), ())), preferred_element_type=F32
        ).astype(BF16)

    def products(b):
        rows = slice(b * 128, b * 128 + 128)
        grad = lax.dot_general(
            tok[:, rows], portion, (((0,), (0,)), ((), ())), preferred_element_type=F32
        )
        fresh = anchor[rows, :] - (wv[rows, :].astype(F32) - inner_rate * grad)
        fbuf[0, rows, :] = fresh.astype(BF16)
        pre[rows, :] = anchor[rows, :] - outer_rate * (
            outer_momentum * outer_momentum * mom[rows, :] + (fresh - stale[rows, :].astype(F32)) * (1.0 / WORKERS)
        )

    def finish(core, o):
        rows = pl.ds(pl.multiple_of(core * HALF + chunk(o), CH), CH)
        nbuf[0, rows, :] = (pre[rows, :] - (outer_rate * (1.0 + outer_momentum)) * full[rows, :]).astype(BF16)

    for s in range(Y // 2):
        for j, way in long_first:
            n = hops(j, way)
            if s < n:
                o = -way * (s + 1)
                here = place(c, o, j)
                got(full.at[here], rid(ID_AG, j, way, s))
                if s + 1 < n:
                    send(full.at[here], full.at[here], rid(ID_AG, j, way, s + 1), ynext[way])
                send(full.at[here], full.at[here], ID_PAG(o % Y, j), partner)
        if s == 0:
            c_anchor.wait()
            c_mom.wait()
        if s < 2:
            products(2 * s)
            products(2 * s + 1)
        if s == 2:
            for o in (0, 1, -1, 2, -2, 3, -3):
                finish(c, o)
            for o in (0, 1, -1, 2, -2):
                for j in range(J):
                    got(full.at[place(1 - c, o, j)], ID_PAG(o % Y, j))
                finish(1 - c, o)
    for k in range(ZH - 1):
        got(zb.at[k], ID_PZ(k))
    keys[...] = ((ksum[zh] + zb[0]) + (zb[1] + zb[2])).astype(BF16)
    finish(c, Y // 2)
    for o in (3, -3, Y // 2):
        for j in range(J):
            got(full.at[place(1 - c, o, j)], ID_PAG(o % Y, j))
        finish(1 - c, o)
    share = pl.ds(pl.multiple_of(w * 8, 8), 8)
    nm[...] = outer_momentum * mom[share, :] + full[share, :]

    for copy in sent:
        copy.wait_send()


def write(*refs):
    n = len(refs) // 2
    copies = [pltpu.make_async_copy(a, b, refs[-1].at[i]) for i, (a, b) in enumerate(zip(refs[:n], refs[n:-1]))]
    for copy in copies:
        copy.start()
    for copy in copies:
        copy.wait()


def local(*args):
    args = [pltpu.with_memory_space_constraint(a, pltpu.HBM) for a in args]
    scratch = [
        pltpu.VMEM((ROWS, KW), BF16),
        pltpu.VMEM((ROWS, KW), BF16),
        pltpu.VMEM((TOK, ROWS), BF16),
        pltpu.VMEM((ROWS, KW), F32),
        pltpu.VMEM((ROWS, KW), F32),
        pltpu.VMEM((HALF, KW), BF16),
        pltpu.VMEM((HALF, KW), F32),
        pltpu.VMEM((J, 2, Y // 2, R, KW), F32),
        pltpu.VMEM((J, ZL, R, KW), F32),
        pltpu.VMEM((ROWS, KW), F32),
        pltpu.VMEM((ROWS, KW), F32),
        pltpu.VMEM((ZH * X, SH, KW), BF16),
        pltpu.VMEM((X, ZH, SH, KW), F32),
        pltpu.VMEM((X - 1, ZH, SH, KW), F32),
        pltpu.VMEM((ZH, SH, KW), F32),
        pltpu.VMEM((3, SH, KW), F32),
        pltpu.SemaphoreType.DMA((N_REMOTE,)),
        pltpu.SemaphoreType.DMA((N_REMOTE,)),
        pltpu.SemaphoreType.DMA((N_LOCAL,)),
        pltpu.SemaphoreType.REGULAR,
        pltpu.SemaphoreType.REGULAR((2,)),
        pltpu.SemaphoreType.REGULAR,
        pltpu.SemaphoreType.REGULAR,
        pltpu.SemaphoreType.REGULAR,
    ]
    hbm = pl.BlockSpec(memory_space=pl.ANY)
    vmem = pl.BlockSpec(memory_space=pltpu.VMEM)
    shapes = (
        jax.ShapeDtypeStruct((SH, KW), BF16),
        jax.ShapeDtypeStruct((TOK, ROWS), BF16),
        jax.ShapeDtypeStruct((1, ROWS, KW), BF16),
        jax.ShapeDtypeStruct((8, KW), F32),
        jax.ShapeDtypeStruct((1, ROWS, KW), BF16),
    )
    results = pl.pallas_call(
        kernel,
        out_shape=shapes,
        in_specs=[hbm] * 6,
        out_specs=(vmem,) * 5,
        scratch_shapes=scratch,
        compiler_params=pltpu.CompilerParams(
            collective_id=0, has_side_effects=True, vmem_limit_bytes=VMEM_LIMIT
        ),
    )(*args)
    return pl.pallas_call(
        write,
        out_shape=shapes,
        in_specs=[vmem] * 5,
        out_specs=(hbm,) * 5,
        scratch_shapes=[pltpu.SemaphoreType.DMA((5,))],
        compiler_params=pltpu.CompilerParams(vmem_limit_bytes=4 * 1024 * 1024),
    )(*results)


def solution(mesh):
    in_specs = (
        P("worker", "fsdp"),
        P("worker", "fsdp", None),
        P(("worker", "fsdp"), None),
        P("fsdp", None),
        P("fsdp", None),
        P("worker", "fsdp", None),
    )
    out_specs = (
        P(("worker", "fsdp"), None),
        P("worker", "fsdp"),
        P("worker", "fsdp", None),
        P(("fsdp", "worker"), None),
        P("worker", "fsdp", None),
    )
    return jax.shard_map(local, mesh=mesh, in_specs=in_specs, out_specs=out_specs, check_vma=False)
```

```python
import jax
import jax.numpy as jnp
from jax import lax
from jax.experimental import pallas as pl
from jax.experimental.pallas import tpu as pltpu
from jax.sharding import PartitionSpec as P

inner_rate = 0.0005
outer_rate = 0.7
outer_momentum = 0.9

Y, ZL, C, ZH, X = 8, 4, 2, 4, 4
WORKERS = Y * ZL * C
ROWS, KW, TOK = 512, 512, 256
HALF = ROWS // C
CH = HALF // Y
J = 2
R = CH // J
SH = 16
VMEM_LIMIT = 40 * 1024 * 1024
F32, BF16 = jnp.float32, jnp.bfloat16
MESH = pl.DeviceIdType.MESH


class Ids:
    def __init__(self):
        self.n = 0

    def __call__(self, *shape):
        first, self.n = self.n, self.n + _size(shape)

        def at(*index):
            k = 0
            for i, s in zip(index, shape):
                k = k * s + i
            return first + k

        return at


def _size(shape):
    n = 1
    for s in shape:
        n *= s
    return n


ids = Ids()
ID_PAIR = ids(Y)
ID_RS = ids(J, 2, Y // 2)
ID_Z = ids(J, ZL)
ID_AG = ids(J, 2, Y // 2)
ID_PAG = ids(Y, J)
ID_KZ = ids(ZH - 1)
ID_KX = ids(4, X - 1)
ID_PX = ids(X - 1)
ID_PZ = ids(ZH - 1)
N_REMOTE = ids.n

loc = Ids()
L_STALE, L_W, L_TOK, L_ANCHOR, L_MOM, L_KG = (loc(1)() for _ in range(6))
N_LOCAL = loc.n


def kernel(
    tok_ref, w_ref, kg_ref, anchor_ref, mom_ref, stale_ref,
    keys, ig, nbuf, nm, fbuf,
    stale, wv, tok, anchor, mom, pair, acc, rs, zbuf, full, pre,
    kg, part, xbuf, ksum, zb,
    ss, rr, ls, ans_c, ans_y, ans_z, ans_x, ans_h,
):
    w = lax.axis_index("worker")
    f = lax.axis_index("fsdp")
    c, zl, y = w % C, (w // C) % ZL, w // (C * ZL)
    x, zh = f % X, f // X

    def dev(y=y, zl=zl, c=c, zh=zh, x=x):
        return ((y * ZL + zl) * C + c, zh * X + x)

    def wrap(v, n):
        return (v + n) % n

    partner = dev(c=1 - c)
    ynext = {1: dev(y=wrap(y + 1, Y)), -1: dev(y=wrap(y - 1, Y))}
    zpeer = [dev(zl=wrap(zl + k, ZL)) for k in range(1, ZL)]
    xpeer = [dev(x=wrap(x + k, X)) for k in range(1, X)]

    zat = [wrap(zl + k, ZL) for k in range(1, ZL)]
    xat = [wrap(x + k, X) for k in range(1, X)]
    hat = [wrap(zh + k, ZH) for k in range(1, ZH)]
    hpeer = [dev(zh=at) for at in hat]
    low = zl < ZL // 2
    end = jnp.where(low, ZL - 1, 0)
    zfar = [end, jnp.where(zl == 0, 2, jnp.where(zl == 1, 0, jnp.where(zl == 2, 3, 1))), jnp.where(low, zl + 1, zl - 1)]
    lower = [at < zh for at in hat]

    odd = y % 2 == 1
    relations = [(partner, c == 1, ans_c)]
    relations += [(ynext[way], odd, ans_y.at[0 if way == -1 else 1]) for way in (1, -1)]
    relations += [(peer, at < zl, ans_z) for peer, at in zip(zpeer, zat)]
    relations += [(peer, at < x, ans_x) for peer, at in zip(xpeer, xat)]
    relations += [(peer, at > zh, ans_h) for peer, at in zip(hpeer, hat)]
    n_greeted = (1 - c) + 2 * (1 - y % 2) + (ZL - 1 - zl) + (X - 1 - x) + zh

    barrier = pltpu.get_barrier_semaphore()
    for peer, greets, _ in relations:

        @pl.when(greets)
        def _():
            pl.semaphore_signal(barrier, inc=1, device_id=peer, device_id_type=MESH)

    def enter():
        @pl.when(n_greeted > 0)
        def _():
            pl.semaphore_wait(barrier, n_greeted)

    def answer_to(some):
        for peer, greets, answer in some:

            @pl.when(jnp.logical_not(greets))
            def _():
                pl.semaphore_signal(answer, inc=1, device_id=peer, device_id_type=MESH)

    def answered(sem, n):
        @pl.when(n > 0)
        def _():
            pl.semaphore_wait(sem, n)

    def load(src, dst, at):
        copy = pltpu.make_async_copy(src, dst, ls.at[at])
        copy.start()
        return copy

    h0, h1 = pl.multiple_of(c * HALF, HALF), pl.multiple_of((1 - c) * HALF, HALF)
    c_stale = load(stale_ref.at[0], stale, L_STALE)
    c_w = load(w_ref.at[0], wv, L_W)
    c_tok = load(tok_ref, tok, L_TOK)
    c_kg = load(kg_ref, kg.at[f], L_KG)
    c_anchor = load(anchor_ref, anchor, L_ANCHOR)
    c_mom = load(mom_ref, mom, L_MOM)

    sent = []

    def send(src, dst, at, to, recv_at=None):
        copy = pltpu.make_async_remote_copy(
            src_ref=src, dst_ref=dst, send_sem=ss.at[at], recv_sem=rr.at[at if recv_at is None else recv_at],
            device_id=to, device_id_type=MESH,
        )
        copy.start()
        sent.append(copy)

    def got(dst, at):
        pltpu.make_async_remote_copy(
            src_ref=dst, dst_ref=dst, send_sem=ss.at[at], recv_sem=rr.at[at],
            device_id=partner, device_id_type=MESH,
        ).wait_recv()

    enter()
    answer_to(relations[:3])
    answered(ans_c, c)

    order = [Y // 2] + [s * k for k in range(Y // 2 - 1, 0, -1) for s in (1, -1)] + [0]

    def chunk(o):
        return pl.multiple_of(wrap(y + o, Y) * CH, CH)

    for i, o in enumerate(order):
        at = chunk(o)
        send(stale_ref.at[0, pl.ds(h1 + at, CH)], pair.at[pl.ds(at, CH)], ID_PAIR(i), partner)

    answer_to(relations[3:])

    c_stale.wait()

    def hops(j, way):
        return Y // 2 if (j % 2 == 0) == (way == 1) else Y // 2 - 1

    def slot(j, way, s):
        return rs.at[j, 0 if way == 1 else 1, s]

    def rid(ident, j, way, s):
        return ident(j, 0 if way == 1 else 1, s)

    long_first = [(j, way) for n in (Y // 2, Y // 2 - 1) for j in range(J) for way in (1, -1) if hops(j, way) == n]
    ways = [1, -1]
    for i, o in enumerate(order):
        at = chunk(o)
        got(pair.at[pl.ds(at, CH)], ID_PAIR(i))
        acc[pl.ds(at, CH), :] = stale[pl.ds(h0 + at, CH), :].astype(F32) + pair[pl.ds(at, CH), :].astype(F32)
        for j, way in long_first:
            if hops(j, way) * way == o or (o == Y // 2 and hops(j, way) == o):
                if way in ways:
                    ways.remove(way)
                    answered(ans_y.at[0 if way == 1 else 1], y % 2)
                send(acc.at[pl.ds(at + j * R, R)], slot(j, way, 0), rid(ID_RS, j, way, 0), ynext[way])

    def kz(k):
        copy = pltpu.make_async_remote_copy(
            src_ref=kg_ref, dst_ref=kg.at[f], send_sem=ss.at[ID_KZ(k)], recv_sem=rr.at[ID_KZ(k)],
            device_id=hpeer[k], device_id_type=MESH,
        )
        return copy

    for k in (1, 0, 2):

        @pl.when(lower[k])
        def _():
            kz(k).start()

        sent.append(kz(k))

    c_w.wait()
    c_tok.wait()
    for b in range(2):
        half = jnp.dot(tok[b * 128 : b * 128 + 128, :], wv[...], preferred_element_type=F32)
        for i in range(8):
            at = b * 8 + i
            part[at % X, at // X] = half[i * SH : (i + 1) * SH]

    for s in range(1, Y // 2):
        for j, way in long_first:
            n = hops(j, way)
            if s < n:
                mine = slot(j, way, s - 1)
                got(mine, rid(ID_RS, j, way, s - 1))
                mine[...] = mine[...] + acc[pl.ds(chunk(way * (n - s)) + j * R, R), :]
                send(mine, slot(j, way, s), rid(ID_RS, j, way, s), ynext[way])
        if s == 1:
            answered(ans_x, x)
            for k in range(X - 1):
                send(kg_ref, kg.at[f], ID_KX(0, k), xpeer[k])
            for k in range(X - 1):
                send(part.at[xat[k]], xbuf.at[k], ID_PX(k), xpeer[k])

    answered(ans_z, zl)
    for j in range(J):
        total = acc[pl.ds(chunk(0) + j * R, R), :]
        for way in (1, -1):
            n = hops(j, way)
            got(slot(j, way, n - 1), rid(ID_RS, j, way, n - 1))
            total = total + slot(j, way, n - 1)[...]
        zbuf[j, zl] = total
        for k in range(ZL - 1):
            send(zbuf.at[j, zl], zbuf.at[j, zl], ID_Z(j, k), dev(zl=zfar[k]), ID_Z(j, 0) + zl)

    answered(ans_h, ZH - 1 - zh)
    for k in (1, 0, 2):

        @pl.when(jnp.logical_not(lower[k]))
        def _():
            kz(k).start()

    for k in range(ZH - 1):
        at = wrap(zh - k - 1, ZH) * X + x
        got(kg.at[at], ID_KZ(k))
        for i in range(X - 1):
            send(kg.at[at], kg.at[at], ID_KX(k + 1, i), xpeer[i])

    def place(core, o, j):
        return pl.ds(pl.multiple_of(core * HALF + chunk(o) + j * R, R), R)

    for j in range(J):
        for k in range(ZL - 1):
            got(zbuf.at[j, zat[k]], ID_Z(j, 0) + zat[k])
        here = place(c, 0, j)
        full[here, :] = ((zbuf[j, 0] + zbuf[j, 1]) + (zbuf[j, 2] + zbuf[j, 3])) * (1.0 / WORKERS)
        for way in (1, -1):
            send(full.at[here], full.at[here], rid(ID_AG, j, way, 0), ynext[way])
        send(full.at[here], full.at[here], ID_PAG(0, j), partner)

    for k in range(X - 1):
        got(xbuf.at[k], ID_PX(k))
    for i in range(ZH):
        ksum[i] = (part[x, i] + xbuf[0, i]) + (xbuf[1, i] + xbuf[2, i])
    for k in (1, 0, 2):
        send(ksum.at[hat[k]], zb.at[k], ID_PZ(k), hpeer[k])

    for rel in range(ZH):
        for k in range(X - 1):
            at = wrap(zh - rel, ZH) * X + wrap(x - k - 1, X)
            got(kg.at[at], ID_KX(rel, k))
    c_kg.wait()
    portion = kg[...].reshape(TOK, KW)
    for b in range(2):
        ig[b * 128 : b * 128 + 128, :] = lax.dot_general(
            portion[b * 128 : b * 128 + 128], wv[...], (((1,), (1,)), ((), ())), preferred_element_type=F32
        ).astype(BF16)

    def products(b):
        rows = slice(b * 128, b * 128 + 128)
        grad = lax.dot_general(
            tok[:, rows], portion, (((0,), (0,)), ((), ())), preferred_element_type=F32
        )
        fresh = anchor[rows, :] - (wv[rows, :].astype(F32) - inner_rate * grad)
        fbuf[0, rows, :] = fresh.astype(BF16)
        pre[rows, :] = anchor[rows, :] - outer_rate * (
            outer_momentum * outer_momentum * mom[rows, :] + (fresh - stale[rows, :].astype(F32)) * (1.0 / WORKERS)
        )

    def finish(core, o):
        rows = pl.ds(pl.multiple_of(core * HALF + chunk(o), CH), CH)
        nbuf[0, rows, :] = (pre[rows, :] - (outer_rate * (1.0 + outer_momentum)) * full[rows, :]).astype(BF16)

    for s in range(Y // 2):
        for j, way in long_first:
            n = hops(j, way)
            if s < n:
                o = -way * (s + 1)
                here = place(c, o, j)
                got(full.at[here], rid(ID_AG, j, way, s))
                if s + 1 < n:
                    send(full.at[here], full.at[here], rid(ID_AG, j, way, s + 1), ynext[way])
                send(full.at[here], full.at[here], ID_PAG(o % Y, j), partner)
        if s == 0:
            c_anchor.wait()
            c_mom.wait()
        if s < 2:
            products(2 * s)
            products(2 * s + 1)
        if s == 2:
            for o in (0, 1, -1, 2, -2, 3, -3):
                finish(c, o)
            for o in (0, 1, -1, 2, -2):
                for j in range(J):
                    got(full.at[place(1 - c, o, j)], ID_PAG(o % Y, j))
                finish(1 - c, o)
    for k in range(ZH - 1):
        got(zb.at[k], ID_PZ(k))
    keys[...] = ((ksum[zh] + zb[0]) + (zb[1] + zb[2])).astype(BF16)
    finish(c, Y // 2)
    for o in (3, -3, Y // 2):
        for j in range(J):
            got(full.at[place(1 - c, o, j)], ID_PAG(o % Y, j))
        finish(1 - c, o)
    share = pl.ds(pl.multiple_of(w * 8, 8), 8)
    nm[...] = outer_momentum * mom[share, :] + full[share, :]

    for copy in sent:
        copy.wait_send()


def write(*refs):
    n = len(refs) // 2
    copies = [pltpu.make_async_copy(a, b, refs[-1].at[i]) for i, (a, b) in enumerate(zip(refs[:n], refs[n:-1]))]
    for copy in copies:
        copy.start()
    for copy in copies:
        copy.wait()


def local(*args):
    args = [pltpu.with_memory_space_constraint(a, pltpu.HBM) for a in args]
    scratch = [
        pltpu.VMEM((ROWS, KW), BF16),
        pltpu.VMEM((ROWS, KW), BF16),
        pltpu.VMEM((TOK, ROWS), BF16),
        pltpu.VMEM((ROWS, KW), F32),
        pltpu.VMEM((ROWS, KW), F32),
        pltpu.VMEM((HALF, KW), BF16),
        pltpu.VMEM((HALF, KW), F32),
        pltpu.VMEM((J, 2, Y // 2, R, KW), F32),
        pltpu.VMEM((J, ZL, R, KW), F32),
        pltpu.VMEM((ROWS, KW), F32),
        pltpu.VMEM((ROWS, KW), F32),
        pltpu.VMEM((ZH * X, SH, KW), BF16),
        pltpu.VMEM((X, ZH, SH, KW), F32),
        pltpu.VMEM((X - 1, ZH, SH, KW), F32),
        pltpu.VMEM((ZH, SH, KW), F32),
        pltpu.VMEM((3, SH, KW), F32),
        pltpu.SemaphoreType.DMA((N_REMOTE,)),
        pltpu.SemaphoreType.DMA((N_REMOTE,)),
        pltpu.SemaphoreType.DMA((N_LOCAL,)),
        pltpu.SemaphoreType.REGULAR,
        pltpu.SemaphoreType.REGULAR((2,)),
        pltpu.SemaphoreType.REGULAR,
        pltpu.SemaphoreType.REGULAR,
        pltpu.SemaphoreType.REGULAR,
    ]
    hbm = pl.BlockSpec(memory_space=pl.ANY)
    vmem = pl.BlockSpec(memory_space=pltpu.VMEM)
    shapes = (
        jax.ShapeDtypeStruct((SH, KW), BF16),
        jax.ShapeDtypeStruct((TOK, ROWS), BF16),
        jax.ShapeDtypeStruct((1, ROWS, KW), BF16),
        jax.ShapeDtypeStruct((8, KW), F32),
        jax.ShapeDtypeStruct((1, ROWS, KW), BF16),
    )
    results = pl.pallas_call(
        kernel,
        out_shape=shapes,
        in_specs=[hbm] * 6,
        out_specs=(vmem,) * 5,
        scratch_shapes=scratch,
        compiler_params=pltpu.CompilerParams(
            collective_id=0, has_side_effects=True, vmem_limit_bytes=VMEM_LIMIT
        ),
    )(*args)
    return pl.pallas_call(
        write,
        out_shape=shapes,
        in_specs=[vmem] * 5,
        out_specs=(hbm,) * 5,
        scratch_shapes=[pltpu.SemaphoreType.DMA((5,))],
        compiler_params=pltpu.CompilerParams(vmem_limit_bytes=4 * 1024 * 1024),
    )(*results)


def solution(mesh):
    in_specs = (
        P("worker", "fsdp"),
        P("worker", "fsdp", None),
        P(("worker", "fsdp"), None),
        P("fsdp", None),
        P("fsdp", None),
        P("worker", "fsdp", None),
    )
    out_specs = (
        P(("worker", "fsdp"), None),
        P("worker", "fsdp"),
        P("worker", "fsdp", None),
        P(("fsdp", "worker"), None),
        P("worker", "fsdp", None),
    )
    return jax.shard_map(local, mesh=mesh, in_specs=in_specs, out_specs=out_specs, check_vma=False)
```

```python
import jax
import jax.numpy as jnp
from jax import lax
from jax.experimental import pallas as pl
from jax.experimental.pallas import tpu as pltpu
from jax.sharding import PartitionSpec as P

inner_rate = 0.0005
outer_rate = 0.7
outer_momentum = 0.9

Y, ZL, C, ZH, X = 8, 4, 2, 4, 4
WORKERS = Y * ZL * C
ROWS, KW, TOK = 512, 512, 256
HALF = ROWS // C
CH = HALF // Y
J = 2
R = CH // J
SH = 16
VMEM_LIMIT = 40 * 1024 * 1024
F32, BF16 = jnp.float32, jnp.bfloat16
MESH = pl.DeviceIdType.MESH


class Ids:
    def __init__(self):
        self.n = 0

    def __call__(self, *shape):
        first, self.n = self.n, self.n + _size(shape)

        def at(*index):
            k = 0
            for i, s in zip(index, shape):
                k = k * s + i
            return first + k

        return at


def _size(shape):
    n = 1
    for s in shape:
        n *= s
    return n


ids = Ids()
ID_PAIR = ids(Y)
ID_RS = ids(J, 2, Y // 2)
ID_Z = ids(J, ZL)
ID_AG = ids(J, 2, Y // 2)
ID_PAG = ids(Y, J)
ID_KZ = ids(ZH - 1)
ID_KX = ids(4, X - 1)
ID_PX = ids(X - 1)
ID_PZ = ids(ZH - 1)
N_REMOTE = ids.n

loc = Ids()
L_STALE, L_W, L_TOK, L_ANCHOR, L_MOM, L_KG = (loc(1)() for _ in range(6))
N_LOCAL = loc.n


def kernel(
    tok_ref, w_ref, kg_ref, anchor_ref, mom_ref, stale_ref,
    keys, ig, nbuf, nm, fbuf,
    stale, wv, tok, anchor, mom, pair, acc, rs, zbuf, full, pre,
    kg, part, xbuf, ksum, zb,
    ss, rr, ls, ans_c, ans_y, ans_z, ans_x, ans_h,
):
    w = lax.axis_index("worker")
    f = lax.axis_index("fsdp")
    c, zl, y = w % C, (w // C) % ZL, w // (C * ZL)
    x, zh = f % X, f // X

    def dev(y=y, zl=zl, c=c, zh=zh, x=x):
        return ((y * ZL + zl) * C + c, zh * X + x)

    def wrap(v, n):
        return (v + n) % n

    partner = dev(c=1 - c)
    ynext = {1: dev(y=wrap(y + 1, Y)), -1: dev(y=wrap(y - 1, Y))}
    zpeer = [dev(zl=wrap(zl + k, ZL)) for k in range(1, ZL)]
    xpeer = [dev(x=wrap(x + k, X)) for k in range(1, X)]

    zat = [wrap(zl + k, ZL) for k in range(1, ZL)]
    xat = [wrap(x + k, X) for k in range(1, X)]
    hat = [wrap(zh + k, ZH) for k in range(1, ZH)]
    hpeer = [dev(zh=at) for at in hat]
    low = zl < ZL // 2
    end = jnp.where(low, ZL - 1, 0)
    zfar = [end, jnp.where(zl == 0, 2, jnp.where(zl == 1, 0, jnp.where(zl == 2, 3, 1))), jnp.where(low, zl + 1, zl - 1)]
    lower = [at < zh for at in hat]

    odd = y % 2 == 1
    relations = [(partner, c == 1, ans_c)]
    relations += [(ynext[way], odd, ans_y.at[0 if way == -1 else 1]) for way in (1, -1)]
    relations += [(peer, at < zl, ans_z) for peer, at in zip(zpeer, zat)]
    relations += [(peer, at < x, ans_x) for peer, at in zip(xpeer, xat)]
    relations += [(peer, at > zh, ans_h) for peer, at in zip(hpeer, hat)]
    n_greeted = (1 - c) + 2 * (1 - y % 2) + (ZL - 1 - zl) + (X - 1 - x) + zh

    barrier = pltpu.get_barrier_semaphore()
    for peer, greets, _ in relations:

        @pl.when(greets)
        def _():
            pl.semaphore_signal(barrier, inc=1, device_id=peer, device_id_type=MESH)

    def enter():
        @pl.when(n_greeted > 0)
        def _():
            pl.semaphore_wait(barrier, n_greeted)

    def answer_to(some):
        for peer, greets, answer in some:

            @pl.when(jnp.logical_not(greets))
            def _():
                pl.semaphore_signal(answer, inc=1, device_id=peer, device_id_type=MESH)

    def answered(sem, n):
        @pl.when(n > 0)
        def _():
            pl.semaphore_wait(sem, n)

    def load(src, dst, at):
        copy = pltpu.make_async_copy(src, dst, ls.at[at])
        copy.start()
        return copy

    h0, h1 = pl.multiple_of(c * HALF, HALF), pl.multiple_of((1 - c) * HALF, HALF)
    c_stale = load(stale_ref.at[0], stale, L_STALE)
    c_w = load(w_ref.at[0], wv, L_W)
    c_tok = load(tok_ref, tok, L_TOK)
    c_kg = load(kg_ref, kg.at[f], L_KG)
    c_anchor = load(anchor_ref, anchor, L_ANCHOR)
    c_mom = load(mom_ref, mom, L_MOM)

    sent = []

    def send(src, dst, at, to, recv_at=None):
        copy = pltpu.make_async_remote_copy(
            src_ref=src, dst_ref=dst, send_sem=ss.at[at], recv_sem=rr.at[at if recv_at is None else recv_at],
            device_id=to, device_id_type=MESH,
        )
        copy.start()
        sent.append(copy)

    def got(dst, at):
        pltpu.make_async_remote_copy(
            src_ref=dst, dst_ref=dst, send_sem=ss.at[at], recv_sem=rr.at[at],
            device_id=partner, device_id_type=MESH,
        ).wait_recv()

    enter()
    answer_to(relations[:3])
    answered(ans_c, c)

    order = [Y // 2] + [s * k for k in range(Y // 2 - 1, 0, -1) for s in (1, -1)] + [0]

    def chunk(o):
        return pl.multiple_of(wrap(y + o, Y) * CH, CH)

    for i, o in enumerate(order):
        at = chunk(o)
        send(stale_ref.at[0, pl.ds(h1 + at, CH)], pair.at[pl.ds(at, CH)], ID_PAIR(i), partner)

    answer_to(relations[3:])

    c_stale.wait()

    def hops(j, way):
        return Y // 2 if (j % 2 == 0) == (way == 1) else Y // 2 - 1

    def slot(j, way, s):
        return rs.at[j, 0 if way == 1 else 1, s]

    def rid(ident, j, way, s):
        return ident(j, 0 if way == 1 else 1, s)

    long_first = [(j, way) for n in (Y // 2, Y // 2 - 1) for j in range(J) for way in (1, -1) if hops(j, way) == n]
    ways = [1, -1]
    for i, o in enumerate(order):
        at = chunk(o)
        got(pair.at[pl.ds(at, CH)], ID_PAIR(i))
        acc[pl.ds(at, CH), :] = stale[pl.ds(h0 + at, CH), :].astype(F32) + pair[pl.ds(at, CH), :].astype(F32)
        for j, way in long_first:
            if hops(j, way) * way == o or (o == Y // 2 and hops(j, way) == o):
                if way in ways:
                    ways.remove(way)
                    answered(ans_y.at[0 if way == 1 else 1], y % 2)
                send(acc.at[pl.ds(at + j * R, R)], slot(j, way, 0), rid(ID_RS, j, way, 0), ynext[way])

    def kz(k):
        copy = pltpu.make_async_remote_copy(
            src_ref=kg_ref, dst_ref=kg.at[f], send_sem=ss.at[ID_KZ(k)], recv_sem=rr.at[ID_KZ(k)],
            device_id=hpeer[k], device_id_type=MESH,
        )
        return copy

    for k in (1, 0, 2):

        @pl.when(lower[k])
        def _():
            kz(k).start()

        sent.append(kz(k))

    c_w.wait()
    c_tok.wait()
    for b in range(2):
        half = jnp.dot(tok[b * 128 : b * 128 + 128, :], wv[...], preferred_element_type=F32)
        for i in range(8):
            at = b * 8 + i
            part[at % X, at // X] = half[i * SH : (i + 1) * SH]

    answered(ans_x, x)
    for k in range(X - 1):
        send(kg_ref, kg.at[f], ID_KX(0, k), xpeer[k])
    for k in range(X - 1):
        send(part.at[xat[k]], xbuf.at[k], ID_PX(k), xpeer[k])

    for s in range(1, Y // 2):
        for j, way in long_first:
            n = hops(j, way)
            if s < n:
                mine = slot(j, way, s - 1)
                got(mine, rid(ID_RS, j, way, s - 1))
                mine[...] = mine[...] + acc[pl.ds(chunk(way * (n - s)) + j * R, R), :]
                send(mine, slot(j, way, s), rid(ID_RS, j, way, s), ynext[way])

    for k in range(X - 1):
        got(xbuf.at[k], ID_PX(k))
    for i in range(ZH):
        ksum[i] = (part[x, i] + xbuf[0, i]) + (xbuf[1, i] + xbuf[2, i])

    def pz(k):
        return pltpu.make_async_remote_copy(
            src_ref=ksum.at[hat[k]], dst_ref=zb.at[k], send_sem=ss.at[ID_PZ(k)], recv_sem=rr.at[ID_PZ(k)],
            device_id=hpeer[k], device_id_type=MESH,
        )

    for k in (1, 0, 2):

        @pl.when(lower[k])
        def _():
            pz(k).start()

        sent.append(pz(k))

    answered(ans_z, zl)
    for j in range(J):
        total = acc[pl.ds(chunk(0) + j * R, R), :]
        for way in (1, -1):
            n = hops(j, way)
            got(slot(j, way, n - 1), rid(ID_RS, j, way, n - 1))
            total = total + slot(j, way, n - 1)[...]
        zbuf[j, zl] = total
        for k in range(ZL - 1):
            send(zbuf.at[j, zl], zbuf.at[j, zl], ID_Z(j, k), dev(zl=zfar[k]), ID_Z(j, 0) + zl)

    answered(ans_h, ZH - 1 - zh)
    for k in (1, 0, 2):

        @pl.when(jnp.logical_not(lower[k]))
        def _():
            kz(k).start()

    for k in range(ZH - 1):
        at = wrap(zh - k - 1, ZH) * X + x
        got(kg.at[at], ID_KZ(k))
        for i in range(X - 1):
            send(kg.at[at], kg.at[at], ID_KX(k + 1, i), xpeer[i])

    def place(core, o, j):
        return pl.ds(pl.multiple_of(core * HALF + chunk(o) + j * R, R), R)

    for j in range(J):
        for k in range(ZL - 1):
            got(zbuf.at[j, zat[k]], ID_Z(j, 0) + zat[k])
        here = place(c, 0, j)
        full[here, :] = ((zbuf[j, 0] + zbuf[j, 1]) + (zbuf[j, 2] + zbuf[j, 3])) * (1.0 / WORKERS)
        for way in (1, -1):
            send(full.at[here], full.at[here], rid(ID_AG, j, way, 0), ynext[way])
        send(full.at[here], full.at[here], ID_PAG(0, j), partner)

    for k in (1, 0, 2):

        @pl.when(jnp.logical_not(lower[k]))
        def _():
            pz(k).start()


    for rel in range(ZH):
        for k in range(X - 1):
            at = wrap(zh - rel, ZH) * X + wrap(x - k - 1, X)
            got(kg.at[at], ID_KX(rel, k))
    c_kg.wait()
    portion = kg[...].reshape(TOK, KW)
    for b in range(2):
        ig[b * 128 : b * 128 + 128, :] = lax.dot_general(
            portion[b * 128 : b * 128 + 128], wv[...], (((1,), (1,)), ((), ())), preferred_element_type=F32
        ).astype(BF16)

    def products(b):
        rows = slice(b * 128, b * 128 + 128)
        grad = lax.dot_general(
            tok[:, rows], portion, (((0,), (0,)), ((), ())), preferred_element_type=F32
        )
        fresh = anchor[rows, :] - (wv[rows, :].astype(F32) - inner_rate * grad)
        fbuf[0, rows, :] = fresh.astype(BF16)
        pre[rows, :] = anchor[rows, :] - outer_rate * (
            outer_momentum * outer_momentum * mom[rows, :] + (fresh - stale[rows, :].astype(F32)) * (1.0 / WORKERS)
        )

    def finish(core, o):
        rows = pl.ds(pl.multiple_of(core * HALF + chunk(o), CH), CH)
        nbuf[0, rows, :] = (pre[rows, :] - (outer_rate * (1.0 + outer_momentum)) * full[rows, :]).astype(BF16)

    for s in range(Y // 2):
        for j, way in long_first:
            n = hops(j, way)
            if s < n:
                o = -way * (s + 1)
                here = place(c, o, j)
                got(full.at[here], rid(ID_AG, j, way, s))
                if s + 1 < n:
                    send(full.at[here], full.at[here], rid(ID_AG, j, way, s + 1), ynext[way])
                send(full.at[here], full.at[here], ID_PAG(o % Y, j), partner)
        if s == 0:
            c_anchor.wait()
            c_mom.wait()
        if s < 2:
            products(2 * s)
            products(2 * s + 1)
        if s == 2:
            for o in (0, 1, -1, 2, -2, 3, -3):
                finish(c, o)
            for o in (0, 1, -1, 2, -2):
                for j in range(J):
                    got(full.at[place(1 - c, o, j)], ID_PAG(o % Y, j))
                finish(1 - c, o)
    for k in range(ZH - 1):
        got(zb.at[k], ID_PZ(k))
    keys[...] = ((ksum[zh] + zb[0]) + (zb[1] + zb[2])).astype(BF16)
    finish(c, Y // 2)
    for o in (3, -3, Y // 2):
        for j in range(J):
            got(full.at[place(1 - c, o, j)], ID_PAG(o % Y, j))
        finish(1 - c, o)
    share = pl.ds(pl.multiple_of(w * 8, 8), 8)
    nm[...] = outer_momentum * mom[share, :] + full[share, :]

    for copy in sent:
        copy.wait_send()


def write(*refs):
    n = len(refs) // 2
    copies = [pltpu.make_async_copy(a, b, refs[-1].at[i]) for i, (a, b) in enumerate(zip(refs[:n], refs[n:-1]))]
    for copy in copies:
        copy.start()
    for copy in copies:
        copy.wait()


def local(*args):
    args = [pltpu.with_memory_space_constraint(a, pltpu.HBM) for a in args]
    scratch = [
        pltpu.VMEM((ROWS, KW), BF16),
        pltpu.VMEM((ROWS, KW), BF16),
        pltpu.VMEM((TOK, ROWS), BF16),
        pltpu.VMEM((ROWS, KW), F32),
        pltpu.VMEM((ROWS, KW), F32),
        pltpu.VMEM((HALF, KW), BF16),
        pltpu.VMEM((HALF, KW), F32),
        pltpu.VMEM((J, 2, Y // 2, R, KW), F32),
        pltpu.VMEM((J, ZL, R, KW), F32),
        pltpu.VMEM((ROWS, KW), F32),
        pltpu.VMEM((ROWS, KW), F32),
        pltpu.VMEM((ZH * X, SH, KW), BF16),
        pltpu.VMEM((X, ZH, SH, KW), F32),
        pltpu.VMEM((X - 1, ZH, SH, KW), F32),
        pltpu.VMEM((ZH, SH, KW), F32),
        pltpu.VMEM((3, SH, KW), F32),
        pltpu.SemaphoreType.DMA((N_REMOTE,)),
        pltpu.SemaphoreType.DMA((N_REMOTE,)),
        pltpu.SemaphoreType.DMA((N_LOCAL,)),
        pltpu.SemaphoreType.REGULAR,
        pltpu.SemaphoreType.REGULAR((2,)),
        pltpu.SemaphoreType.REGULAR,
        pltpu.SemaphoreType.REGULAR,
        pltpu.SemaphoreType.REGULAR,
    ]
    hbm = pl.BlockSpec(memory_space=pl.ANY)
    vmem = pl.BlockSpec(memory_space=pltpu.VMEM)
    shapes = (
        jax.ShapeDtypeStruct((SH, KW), BF16),
        jax.ShapeDtypeStruct((TOK, ROWS), BF16),
        jax.ShapeDtypeStruct((1, ROWS, KW), BF16),
        jax.ShapeDtypeStruct((8, KW), F32),
        jax.ShapeDtypeStruct((1, ROWS, KW), BF16),
    )
    results = pl.pallas_call(
        kernel,
        out_shape=shapes,
        in_specs=[hbm] * 6,
        out_specs=(vmem,) * 5,
        scratch_shapes=scratch,
        compiler_params=pltpu.CompilerParams(
            collective_id=0, has_side_effects=True, vmem_limit_bytes=VMEM_LIMIT
        ),
    )(*args)
    return pl.pallas_call(
        write,
        out_shape=shapes,
        in_specs=[vmem] * 5,
        out_specs=(hbm,) * 5,
        scratch_shapes=[pltpu.SemaphoreType.DMA((5,))],
        compiler_params=pltpu.CompilerParams(vmem_limit_bytes=4 * 1024 * 1024),
    )(*results)


def solution(mesh):
    in_specs = (
        P("worker", "fsdp"),
        P("worker", "fsdp", None),
        P(("worker", "fsdp"), None),
        P("fsdp", None),
        P("fsdp", None),
        P("worker", "fsdp", None),
    )
    out_specs = (
        P(("worker", "fsdp"), None),
        P("worker", "fsdp"),
        P("worker", "fsdp", None),
        P(("fsdp", "worker"), None),
        P("worker", "fsdp", None),
    )
    return jax.shard_map(local, mesh=mesh, in_specs=in_specs, out_specs=out_specs, check_vma=False)
```

```python
import jax
import jax.numpy as jnp
from jax import lax
from jax.experimental import pallas as pl
from jax.experimental.pallas import tpu as pltpu
from jax.sharding import PartitionSpec as P

inner_rate = 0.0005
outer_rate = 0.7
outer_momentum = 0.9

Y, ZL, C, ZH, X = 8, 4, 2, 4, 4
WORKERS = Y * ZL * C
ROWS, KW, TOK = 512, 512, 256
HALF = ROWS // C
CH = HALF // Y
J = 2
R = CH // J
SH = 16
VMEM_LIMIT = 40 * 1024 * 1024
F32, BF16 = jnp.float32, jnp.bfloat16
MESH = pl.DeviceIdType.MESH


class Ids:
    def __init__(self):
        self.n = 0

    def __call__(self, *shape):
        first, self.n = self.n, self.n + _size(shape)

        def at(*index):
            k = 0
            for i, s in zip(index, shape):
                k = k * s + i
            return first + k

        return at


def _size(shape):
    n = 1
    for s in shape:
        n *= s
    return n


ids = Ids()
ID_PAIR = ids(Y)
ID_RS = ids(J, 2, Y // 2)
ID_Z = ids(J, ZL)
ID_AG = ids(J, 2, Y // 2)
ID_PAG = ids(Y, J)
ID_KZ = ids(ZH - 1)
ID_KX = ids(4, X - 1)
ID_PX = ids(X - 1)
ID_PZ = ids(ZH - 1)
N_REMOTE = ids.n

loc = Ids()
L_STALE, L_W, L_TOK, L_ANCHOR, L_MOM, L_KG = (loc(1)() for _ in range(6))
N_LOCAL = loc.n


def kernel(
    tok_ref, w_ref, kg_ref, anchor_ref, mom_ref, stale_ref,
    keys, ig, nbuf, nm, fbuf,
    stale, wv, tok, anchor, mom, pair, acc, rs, zbuf, full, pre,
    kg, part, xbuf, ksum, zb,
    ss, rr, ls, ans_c, ans_y, ans_z, ans_x, ans_h,
):
    w = lax.axis_index("worker")
    f = lax.axis_index("fsdp")
    c, zl, y = w % C, (w // C) % ZL, w // (C * ZL)
    x, zh = f % X, f // X

    def dev(y=y, zl=zl, c=c, zh=zh, x=x):
        return ((y * ZL + zl) * C + c, zh * X + x)

    def wrap(v, n):
        return (v + n) % n

    partner = dev(c=1 - c)
    ynext = {1: dev(y=wrap(y + 1, Y)), -1: dev(y=wrap(y - 1, Y))}
    zpeer = [dev(zl=wrap(zl + k, ZL)) for k in range(1, ZL)]
    xpeer = [dev(x=wrap(x + k, X)) for k in range(1, X)]

    zat = [wrap(zl + k, ZL) for k in range(1, ZL)]
    xat = [wrap(x + k, X) for k in range(1, X)]
    hat = [wrap(zh + k, ZH) for k in range(1, ZH)]
    hpeer = [dev(zh=at) for at in hat]
    low = zl < ZL // 2
    end = jnp.where(low, ZL - 1, 0)
    zfar = [end, jnp.where(zl == 0, 2, jnp.where(zl == 1, 0, jnp.where(zl == 2, 3, 1))), jnp.where(low, zl + 1, zl - 1)]
    lower = [at < zh for at in hat]

    odd = y % 2 == 1
    relations = [(partner, c == 1, ans_c)]
    relations += [(ynext[way], odd, ans_y.at[0 if way == -1 else 1]) for way in (1, -1)]
    relations += [(peer, at < zl, ans_z) for peer, at in zip(zpeer, zat)]
    relations += [(peer, at < x, ans_x) for peer, at in zip(xpeer, xat)]
    relations += [(peer, at > zh, ans_h) for peer, at in zip(hpeer, hat)]
    n_greeted = (1 - c) + 2 * (1 - y % 2) + (ZL - 1 - zl) + (X - 1 - x) + zh

    barrier = pltpu.get_barrier_semaphore()
    for peer, greets, _ in relations:

        @pl.when(greets)
        def _():
            pl.semaphore_signal(barrier, inc=1, device_id=peer, device_id_type=MESH)

    def enter():
        @pl.when(n_greeted > 0)
        def _():
            pl.semaphore_wait(barrier, n_greeted)

    def answer_to(some):
        for peer, greets, answer in some:

            @pl.when(jnp.logical_not(greets))
            def _():
                pl.semaphore_signal(answer, inc=1, device_id=peer, device_id_type=MESH)

    def answered(sem, n):
        @pl.when(n > 0)
        def _():
            pl.semaphore_wait(sem, n)

    def load(src, dst, at):
        copy = pltpu.make_async_copy(src, dst, ls.at[at])
        copy.start()
        return copy

    h0, h1 = pl.multiple_of(c * HALF, HALF), pl.multiple_of((1 - c) * HALF, HALF)
    c_stale = load(stale_ref.at[0], stale, L_STALE)
    c_w = load(w_ref.at[0], wv, L_W)
    c_tok = load(tok_ref, tok, L_TOK)
    c_kg = load(kg_ref, kg.at[f], L_KG)
    c_anchor = load(anchor_ref, anchor, L_ANCHOR)
    c_mom = load(mom_ref, mom, L_MOM)

    sent = []

    def send(src, dst, at, to, recv_at=None):
        copy = pltpu.make_async_remote_copy(
            src_ref=src, dst_ref=dst, send_sem=ss.at[at], recv_sem=rr.at[at if recv_at is None else recv_at],
            device_id=to, device_id_type=MESH,
        )
        copy.start()
        sent.append(copy)

    def got(dst, at):
        pltpu.make_async_remote_copy(
            src_ref=dst, dst_ref=dst, send_sem=ss.at[at], recv_sem=rr.at[at],
            device_id=partner, device_id_type=MESH,
        ).wait_recv()

    enter()
    answer_to(relations[:3])
    answered(ans_c, c)

    order = [Y // 2] + [s * k for k in range(Y // 2 - 1, 0, -1) for s in (1, -1)] + [0]

    def chunk(o):
        return pl.multiple_of(wrap(y + o, Y) * CH, CH)

    for i, o in enumerate(order):
        at = chunk(o)
        send(stale_ref.at[0, pl.ds(h1 + at, CH)], pair.at[pl.ds(at, CH)], ID_PAIR(i), partner)

    answer_to(relations[3:])

    c_stale.wait()

    def hops(j, way):
        return Y // 2 if (j % 2 == 0) == (way == 1) else Y // 2 - 1

    def slot(j, way, s):
        return rs.at[j, 0 if way == 1 else 1, s]

    def rid(ident, j, way, s):
        return ident(j, 0 if way == 1 else 1, s)

    long_first = [(j, way) for n in (Y // 2, Y // 2 - 1) for j in range(J) for way in (1, -1) if hops(j, way) == n]
    ways = [1, -1]
    for i, o in enumerate(order):
        at = chunk(o)
        got(pair.at[pl.ds(at, CH)], ID_PAIR(i))
        acc[pl.ds(at, CH), :] = stale[pl.ds(h0 + at, CH), :].astype(F32) + pair[pl.ds(at, CH), :].astype(F32)
        for j, way in long_first:
            if hops(j, way) * way == o or (o == Y // 2 and hops(j, way) == o):
                if way in ways:
                    ways.remove(way)
                    answered(ans_y.at[0 if way == 1 else 1], y % 2)
                send(acc.at[pl.ds(at + j * R, R)], slot(j, way, 0), rid(ID_RS, j, way, 0), ynext[way])

    def kz(k):
        copy = pltpu.make_async_remote_copy(
            src_ref=kg_ref, dst_ref=kg.at[f], send_sem=ss.at[ID_KZ(k)], recv_sem=rr.at[ID_KZ(k)],
            device_id=hpeer[k], device_id_type=MESH,
        )
        return copy

    for k in (1, 0, 2):

        @pl.when(lower[k])
        def _():
            kz(k).start()

        sent.append(kz(k))

    c_w.wait()
    c_tok.wait()
    for b in range(2):
        half = jnp.dot(tok[b * 128 : b * 128 + 128, :], wv[...], preferred_element_type=F32)
        for i in range(8):
            at = b * 8 + i
            part[at % X, at // X] = half[i * SH : (i + 1) * SH]

    answered(ans_x, x)
    for k in range(X - 1):
        send(kg_ref, kg.at[f], ID_KX(0, k), xpeer[k])
    for k in range(X - 1):
        send(part.at[xat[k]], xbuf.at[k], ID_PX(k), xpeer[k])

    for s in range(1, Y // 2):
        for j, way in long_first:
            n = hops(j, way)
            if s < n:
                mine = slot(j, way, s - 1)
                got(mine, rid(ID_RS, j, way, s - 1))
                mine[...] = mine[...] + acc[pl.ds(chunk(way * (n - s)) + j * R, R), :]
                send(mine, slot(j, way, s), rid(ID_RS, j, way, s), ynext[way])

    for k in range(X - 1):
        got(xbuf.at[k], ID_PX(k))
    for i in range(ZH):
        ksum[i] = (part[x, i] + xbuf[0, i]) + (xbuf[1, i] + xbuf[2, i])

    def pz(k):
        return pltpu.make_async_remote_copy(
            src_ref=ksum.at[hat[k]], dst_ref=zb.at[k], send_sem=ss.at[ID_PZ(k)], recv_sem=rr.at[ID_PZ(k)],
            device_id=hpeer[k], device_id_type=MESH,
        )

    for k in (1, 0, 2):

        @pl.when(lower[k])
        def _():
            pz(k).start()

        sent.append(pz(k))

    answered(ans_z, zl)
    for j in range(J):
        total = acc[pl.ds(chunk(0) + j * R, R), :]
        for way in (1, -1):
            n = hops(j, way)
            got(slot(j, way, n - 1), rid(ID_RS, j, way, n - 1))
            total = total + slot(j, way, n - 1)[...]
        zbuf[j, zl] = total
        for k in range(ZL - 1):
            send(zbuf.at[j, zl], zbuf.at[j, zl], ID_Z(j, k), dev(zl=zfar[k]), ID_Z(j, 0) + zl)

    answered(ans_h, ZH - 1 - zh)
    for k in (1, 0, 2):

        @pl.when(jnp.logical_not(lower[k]))
        def _():
            kz(k).start()

    def place(core, o, j):
        return pl.ds(pl.multiple_of(core * HALF + chunk(o) + j * R, R), R)

    for j in range(J):
        for k in range(ZL - 1):
            got(zbuf.at[j, zat[k]], ID_Z(j, 0) + zat[k])
        here = place(c, 0, j)
        full[here, :] = ((zbuf[j, 0] + zbuf[j, 1]) + (zbuf[j, 2] + zbuf[j, 3])) * (1.0 / WORKERS)
        for way in (1, -1):
            send(full.at[here], full.at[here], rid(ID_AG, j, way, 0), ynext[way])
        send(full.at[here], full.at[here], ID_PAG(0, j), partner)

    for k in (1, 0, 2):

        @pl.when(jnp.logical_not(lower[k]))
        def _():
            pz(k).start()


    for k in range(ZH - 1):
        at = wrap(zh - k - 1, ZH) * X + x
        got(kg.at[at], ID_KZ(k))
        for i in range(X - 1):
            send(kg.at[at], kg.at[at], ID_KX(k + 1, i), xpeer[i])

    def first_products():
        for rel in range(ZH):
            for k in range(X - 1):
                at = wrap(zh - rel, ZH) * X + wrap(x - k - 1, X)
                got(kg.at[at], ID_KX(rel, k))
        c_kg.wait()
        portion = kg[...].reshape(TOK, KW)
        for b in range(2):
            ig[b * 128 : b * 128 + 128, :] = lax.dot_general(
                portion[b * 128 : b * 128 + 128], wv[...], (((1,), (1,)), ((), ())), preferred_element_type=F32
            ).astype(BF16)

    def products(b):
        rows = slice(b * 128, b * 128 + 128)
        grad = lax.dot_general(
            tok[:, rows], kg[...].reshape(TOK, KW), (((0,), (0,)), ((), ())), preferred_element_type=F32
        )
        fresh = anchor[rows, :] - (wv[rows, :].astype(F32) - inner_rate * grad)
        fbuf[0, rows, :] = fresh.astype(BF16)
        pre[rows, :] = anchor[rows, :] - outer_rate * (
            outer_momentum * outer_momentum * mom[rows, :] + (fresh - stale[rows, :].astype(F32)) * (1.0 / WORKERS)
        )

    def finish(core, o):
        rows = pl.ds(pl.multiple_of(core * HALF + chunk(o), CH), CH)
        nbuf[0, rows, :] = (pre[rows, :] - (outer_rate * (1.0 + outer_momentum)) * full[rows, :]).astype(BF16)

    for s in range(Y // 2):
        for j, way in long_first:
            n = hops(j, way)
            if s < n:
                o = -way * (s + 1)
                here = place(c, o, j)
                got(full.at[here], rid(ID_AG, j, way, s))
                if s + 1 < n:
                    send(full.at[here], full.at[here], rid(ID_AG, j, way, s + 1), ynext[way])
                send(full.at[here], full.at[here], ID_PAG(o % Y, j), partner)
        if s == 1:
            first_products()
            c_anchor.wait()
            c_mom.wait()
        if s == 2:
            for b in range(4):
                products(b)
            for o in (0, 1, -1, 2, -2, 3, -3):
                finish(c, o)
            for o in (0, 1, -1, 2, -2):
                for j in range(J):
                    got(full.at[place(1 - c, o, j)], ID_PAG(o % Y, j))
                finish(1 - c, o)
    for k in range(ZH - 1):
        got(zb.at[k], ID_PZ(k))
    keys[...] = ((ksum[zh] + zb[0]) + (zb[1] + zb[2])).astype(BF16)
    finish(c, Y // 2)
    for o in (3, -3, Y // 2):
        for j in range(J):
            got(full.at[place(1 - c, o, j)], ID_PAG(o % Y, j))
        finish(1 - c, o)
    share = pl.ds(pl.multiple_of(w * 8, 8), 8)
    nm[...] = outer_momentum * mom[share, :] + full[share, :]

    for copy in sent:
        copy.wait_send()


def write(*refs):
    n = len(refs) // 2
    copies = [pltpu.make_async_copy(a, b, refs[-1].at[i]) for i, (a, b) in enumerate(zip(refs[:n], refs[n:-1]))]
    for copy in copies:
        copy.start()
    for copy in copies:
        copy.wait()


def local(*args):
    args = [pltpu.with_memory_space_constraint(a, pltpu.HBM) for a in args]
    scratch = [
        pltpu.VMEM((ROWS, KW), BF16),
        pltpu.VMEM((ROWS, KW), BF16),
        pltpu.VMEM((TOK, ROWS), BF16),
        pltpu.VMEM((ROWS, KW), F32),
        pltpu.VMEM((ROWS, KW), F32),
        pltpu.VMEM((HALF, KW), BF16),
        pltpu.VMEM((HALF, KW), F32),
        pltpu.VMEM((J, 2, Y // 2, R, KW), F32),
        pltpu.VMEM((J, ZL, R, KW), F32),
        pltpu.VMEM((ROWS, KW), F32),
        pltpu.VMEM((ROWS, KW), F32),
        pltpu.VMEM((ZH * X, SH, KW), BF16),
        pltpu.VMEM((X, ZH, SH, KW), F32),
        pltpu.VMEM((X - 1, ZH, SH, KW), F32),
        pltpu.VMEM((ZH, SH, KW), F32),
        pltpu.VMEM((3, SH, KW), F32),
        pltpu.SemaphoreType.DMA((N_REMOTE,)),
        pltpu.SemaphoreType.DMA((N_REMOTE,)),
        pltpu.SemaphoreType.DMA((N_LOCAL,)),
        pltpu.SemaphoreType.REGULAR,
        pltpu.SemaphoreType.REGULAR((2,)),
        pltpu.SemaphoreType.REGULAR,
        pltpu.SemaphoreType.REGULAR,
        pltpu.SemaphoreType.REGULAR,
    ]
    hbm = pl.BlockSpec(memory_space=pl.ANY)
    vmem = pl.BlockSpec(memory_space=pltpu.VMEM)
    shapes = (
        jax.ShapeDtypeStruct((SH, KW), BF16),
        jax.ShapeDtypeStruct((TOK, ROWS), BF16),
        jax.ShapeDtypeStruct((1, ROWS, KW), BF16),
        jax.ShapeDtypeStruct((8, KW), F32),
        jax.ShapeDtypeStruct((1, ROWS, KW), BF16),
    )
    results = pl.pallas_call(
        kernel,
        out_shape=shapes,
        in_specs=[hbm] * 6,
        out_specs=(vmem,) * 5,
        scratch_shapes=scratch,
        compiler_params=pltpu.CompilerParams(
            collective_id=0, has_side_effects=True, vmem_limit_bytes=VMEM_LIMIT
        ),
    )(*args)
    return pl.pallas_call(
        write,
        out_shape=shapes,
        in_specs=[vmem] * 5,
        out_specs=(hbm,) * 5,
        scratch_shapes=[pltpu.SemaphoreType.DMA((5,))],
        compiler_params=pltpu.CompilerParams(vmem_limit_bytes=4 * 1024 * 1024),
    )(*results)


def solution(mesh):
    in_specs = (
        P("worker", "fsdp"),
        P("worker", "fsdp", None),
        P(("worker", "fsdp"), None),
        P("fsdp", None),
        P("fsdp", None),
        P("worker", "fsdp", None),
    )
    out_specs = (
        P(("worker", "fsdp"), None),
        P("worker", "fsdp"),
        P("worker", "fsdp", None),
        P(("fsdp", "worker"), None),
        P("worker", "fsdp", None),
    )
    return jax.shard_map(local, mesh=mesh, in_specs=in_specs, out_specs=out_specs, check_vma=False)
```
